512 devices in a mesh: dp: 8 (over z_lo), mp: 64 (over x, z_hi, y, core).
Axes of the slice: x: 4, y: 4, z: 16 (z_hi: 2, z_lo: 8; z = z_hi * 8 + z_lo), core: 2. Of those that a mesh axis runs over, the one named last changes fastest.
Arguments:
- base_rows: bfloat16 [1024, 8192], P('dp', 'mp'), may hold values from -6 to 6
- layer_rows: bfloat16 [1024, 8192], P('dp', 'mp'), may hold values from -6 to 6
- cross_weight: bfloat16 [8192, 8192], P(None, 'mp'), may hold values from -0.0625 to 0.0625
- cross_bias: float32 [8192], P('mp'), may hold values from -3 to 3
- upstream: bfloat16 [1024, 8192], P('dp', 'mp'), may hold values from -6 to 6
Outputs:
- crossed: bfloat16 [1024, 8192], P('dp', 'mp')
- grad_base: bfloat16 [1024, 8192], P('dp', 'mp')
- grad_layer: bfloat16 [1024, 8192], P('dp', 'mp')
- grad_weight: float32 [8192, 8192], P('dp', 'mp')
- grad_bias: float32 [8192], P('mp')
The draws below stay inside these ranges and needn't reach their ends.
All inputs are finite; a program needn't handle non-finite values.
Results may differ from the reference program's by a relative error of at most 0.0041.
Values may be sent and summed in bfloat16 or wider, within the bound.
A program may use at most 64 MiB of HBM per device.

```python
import jax
import jax.numpy as jnp

D = 8192
BATCH = 1024


def block_scale(key, extent, pieces, least, largest):
    level = 1.0
    for axis_at, blocks in pieces:
        heights = jax.random.uniform(jax.random.fold_in(jax.random.fold_in(key, 6), axis_at), (blocks,), jnp.float32, least / len(pieces), largest / len(pieces))
        level = level * jnp.repeat(jnp.exp(heights), extent[axis_at] // blocks).reshape((-1,) + (1,) * (len(extent) - 1 - axis_at))
    return level


def centred(rng, extent, spread, limit, split=(), dtype=jnp.bfloat16):
    array = jax.random.normal(rng, extent, jnp.float32) * spread
    if len(split) > 0:
        array = block_scale(rng, extent, split, -0.22, 0.18) * array
    return jnp.clip(array, min=-limit, max=limit).astype(dtype)


def setup_inputs(seed: int = 0) -> dict:
    splits = jax.random.split(jax.random.key(seed), 6)
    return {
        "base_rows": centred(splits[0], (BATCH, D), 1.0, 6.0, ((0, 8), (1, 64))),
        "layer_rows": centred(splits[1], (BATCH, D), 1.0, 6.0, ((0, 8), (1, 64))),
        "cross_weight": centred(splits[2], (D, D), D ** -0.5, 0.0625, ((1, 64),)),
        "cross_bias": centred(splits[3], (D,), 0.5, 3.0, ((0, 64),), jnp.float32),
        "upstream": centred(splits[4], (BATCH, D), 1.0, 6.0, ((0, 8), (1, 64))),
    }


def reference(base_rows, layer_rows, cross_weight, cross_bias, upstream):
    mixed = jnp.dot(layer_rows, cross_weight, preferred_element_type=jnp.float32) + cross_bias
    base = base_rows.astype(jnp.float32)
    crossed = (base * mixed + layer_rows.astype(jnp.float32)).astype(jnp.bfloat16)
    upper = upstream.astype(jnp.float32)
    delta = upper * base
    delta_low = delta.astype(jnp.bfloat16)
    grad_base = (upper * mixed).astype(jnp.bfloat16)
    back = jnp.dot(delta_low, cross_weight.T, preferred_element_type=jnp.float32)
    grad_layer = (upper + back).astype(jnp.bfloat16)
    scale = jnp.float32(BATCH) ** -0.5
    grad_weight = jnp.dot(layer_rows.T, delta_low, preferred_element_type=jnp.float32) * scale
    grad_bias = jnp.sum(delta, axis=0) * scale
    return crossed, grad_base, grad_layer, grad_weight, grad_bias
```

```python
import functools

import jax
import jax.numpy as jnp
from jax import lax
from jax.experimental import pallas as pl
from jax.experimental.pallas import tpu as pltpu
from jax.sharding import PartitionSpec as P

MESH = pl.DeviceIdType.MESH
F32 = jnp.float32
BF16 = jnp.bfloat16
N_SEMS = 128


def kernel(
    scale,
    base,
    lay,
    up,
    bias,
    w4,
    crossed,
    gbase,
    glayer,
    gw,
    gbias,
    wo,
    wp,
    dl,
    dlp,
    xa,
    fs,
    xb,
    do,
    dp_,
    bs,
    part,
    r1lo,
    r1hi,
    rl,
    rr,
    s1,
    b2,
    r2,
    tt,
    zs,
    zr,
    mixp,
    mixr,
    gws,
    send,
    recv,
    lsem,
):
    d = lax.axis_index("dp")
    m = lax.axis_index("mp")
    c = lax.rem(m, 2)
    y = lax.rem(lax.div(m, 2), 4)
    h = lax.rem(lax.div(m, 8), 2)
    x = lax.div(m, 16)
    oh = 1 - h
    oc = 1 - c

    def dev(x_=None, y_=None, h_=None, c_=None, d_=None):
        x_ = x if x_ is None else x_
        y_ = y if y_ is None else y_
        h_ = h if h_ is None else h_
        c_ = c if c_ is None else c_
        d_ = d if d_ is None else d_
        return (d_, ((x_ * 2 + h_) * 4 + y_) * 2 + c_)

    def plus(v, k):
        return lax.rem(v + k, 4)

    ids = iter(range(N_SEMS))
    sent = []

    def put(src, dst, to, k=None):
        k = next(ids) if k is None else k
        copy = pltpu.make_async_remote_copy(
            src_ref=src,
            dst_ref=dst,
            send_sem=send.at[k],
            recv_sem=recv.at[k],
            device_id=to,
            device_id_type=MESH,
        )
        copy.start()
        sent.append(copy)
        return k

    def got(k, landed):
        pltpu.make_async_remote_copy(
            src_ref=landed,
            dst_ref=landed,
            send_sem=send.at[k],
            recv_sem=recv.at[k],
            device_id=dev(c_=oc),
            device_id_type=MESH,
        ).wait_recv()

    load_w = pltpu.make_async_copy(w4.at[:, c], wo, lsem.at[0])
    load_w.start()
    own_x = pltpu.make_async_copy(lay, xa.at[h, x, y], lsem.at[1])
    own_x.start()

    barrier = pltpu.get_barrier_semaphore()
    near = [dev(c_=oc)]
    near += [dev(x_=plus(x, k)) for k in (1, 2, 3)]
    near += [dev(y_=plus(y, k)) for k in (1, 2, 3)]
    z = h * 8 + d
    for k in range(1, 16):
        zk = lax.rem(z + k, 16)
        near.append(dev(h_=lax.div(zk, 8), d_=lax.rem(zk, 8)))
    for to in near:
        pl.semaphore_signal(barrier, inc=1, device_id=to, device_id_type=MESH)

    upper = up[...].astype(F32)
    basef = base[...].astype(F32)
    delta = upper * basef
    low = delta.astype(BF16).reshape(4, 32, 128)
    dl[...] = low
    do[:, d] = low
    bs[d] = jnp.broadcast_to(jnp.sum(delta, axis=0, keepdims=True), (8, 128))

    own_x.wait()
    pl.semaphore_wait(barrier, len(near))

    k_dlp = put(dl, dlp, dev(c_=oc))
    k_wp = [
        put(w4.at[pl.ds(8 * j, 8), oc], wp.at[pl.ds(8 * j, 8)], dev(c_=oc))
        for j in range(4)
    ]
    k_zx = put(lay, xa.at[h, x, y], dev(h_=oh))

    def ag1(view, n):
        half = n // 2
        ks = []
        for j in (1, 3, 2):
            a = view(x, y, 0, half)
            b = view(x, y, half, half)
            ka = put(a, a, dev(x_=plus(x, j)))
            kb = put(b, b, dev(y_=plus(y, j)))
            ks.append((j, ka, kb))
        return ks

    def ag1_wait(view, n, ks):
        half = n // 2
        for j, ka, kb in ks:
            got(ka, view(plus(x, 4 - j), y, 0, half))
            got(kb, view(x, plus(y, 4 - j), half, half))

    every = pl.ds(0, 4)

    def ag2(view, n):
        half = n // 2
        ks = []
        for j in (1, 3):
            a = view(every, y, 0, half)
            b = view(x, every, half, half)
            ks.append((put(a, a, dev(y_=plus(y, j))), put(b, b, dev(x_=plus(x, j)))))
        return ks

    def ag2_forward(view, n, ks):
        half = n // 2
        out = []
        for (ka, kb), j, part_of in zip(ks, (1, 3), (pl.ds(0, 2), pl.ds(2, 2)), strict=True):
            ys, xs = plus(y, 4 - j), plus(x, 4 - j)
            got(ka, view(every, ys, 0, half))
            a = view(part_of, ys, 0, half)
            fa = put(a, a, dev(y_=plus(y, j)))
            got(kb, view(xs, every, half, half))
            b = view(xs, part_of, half, half)
            fb = put(b, b, dev(x_=plus(x, j)))
            out.append((fa, fb, part_of))
        return out

    def ag2_wait(view, n, ks):
        half = n // 2
        for fa, fb, part_of in ks:
            got(fa, view(part_of, plus(y, 2), 0, half))
            got(fb, view(plus(x, 2), part_of, half, half))

    def x_own(xs, ys, q, nq):
        return xa.at[h, xs, ys, pl.ds(q, nq)]

    def x_other(xs, ys, q, nq):
        return xa.at[oh, xs, ys, pl.ds(q, nq)]

    def x_block(xs, ys, q, nq):
        return xb.at[xs, ys, pl.ds(q, nq)]

    own1 = ag1(x_own, 4)

    k_fs = []
    for j in (1, 2, 3):
        t = plus(x, j)
        k_fs.append(put(lay.at[t], fs.at[x], dev(x_=t)))
    for j, k in zip((1, 2, 3), k_fs, strict=True):
        got(k, fs.at[plus(x, 4 - j)])
    z_first = [next(ids) for _ in range(8)]
    z_recv = z_first[0]
    z_sent = []
    for j in range(4):
        for hh in (0, 1):
            s = plus(x, j)
            src = lay.at[x] if j == 0 else fs.at[s]
            d_to = 2 * s + h
            mine = jnp.logical_and(h == hh, d_to == d)
            dst = xb.at[x, y, d]
            copy = pltpu.make_async_remote_copy(
                src_ref=src,
                dst_ref=dst,
                send_sem=send.at[z_first[2 * j + hh]],
                recv_sem=recv.at[z_recv + d],
                device_id=dev(h_=hh, d_=d_to),
                device_id_type=MESH,
            )
            stay = pltpu.make_async_copy(src, dst, recv.at[z_recv + d])

            @pl.when(mine)
            def _(stay=stay):
                stay.start()

            @pl.when(jnp.logical_not(mine))
            def _(copy=copy):
                copy.start()

            z_sent.append((mine, copy))

    k_do = []
    for j in range(1, 8):
        t = lax.rem(d + j, 8)
        kd = put(dl, do.at[:, d], dev(d_=t))
        kb = put(bs.at[d], bs.at[d], dev(d_=t))
        k_do.append((j, kd, kb))

    ag1_wait(x_own, 4, own1)
    own2 = ag2(x_own, 4)

    load_w.wait()
    got(k_dlp, dlp)
    d_own = dl[...].reshape(128, 128)
    d_other = dlp[...].reshape(128, 128)
    nt = (((1,), (1,)), ((), ()))
    for i in range(8):
        if i % 2 == 0:
            got(k_wp[i // 2], wp.at[pl.ds(4 * i, 8)])
        xs, hs = i // 2, i % 2
        term = lax.dot_general(
            wo[4 * i : 4 * i + 4].reshape(512, 128), d_own, nt, preferred_element_type=F32
        ) + lax.dot_general(
            wp[4 * i : 4 * i + 4].reshape(512, 128), d_other, nt, preferred_element_type=F32
        )
        term = term.astype(BF16).reshape(4, 128, 128)
        part[0, xs, :, hs] = term[:, 0:64]
        for ys in range(4):
            part[1, ys, xs, hs] = term[ys, 64:128]

    lo, hi = pl.ds(0, 2), pl.ds(2, 2)

    def to_line(half, j):
        return dev(x_=plus(x, j)) if half == 0 else dev(y_=plus(y, j))

    def to_line2(half, j):
        return dev(y_=plus(y, j)) if half == 0 else dev(x_=plus(x, j))

    k_rs = []
    for half in (0, 1):
        me = x if half == 0 else y
        a = put(part.at[half, plus(me, 2), lo], r1lo.at[half], to_line(half, 1))
        b = put(part.at[half, plus(me, 2), hi], r1hi.at[half], to_line(half, 3))
        e = put(part.at[half, plus(me, 1), hi], rl.at[half, hi], to_line(half, 1))
        f = put(part.at[half, plus(me, 3), lo], rr.at[half, lo], to_line(half, 3))
        k_rs.append((a, b, e, f))

    own3 = ag2_forward(x_own, 4, own2)

    k_rs2 = []
    for half in (0, 1):
        me = x if half == 0 else y
        a, b, _, _ = k_rs[half]
        got(a, r1lo.at[half])
        t = plus(me, 1)
        part[half, t, lo] = (part[half, t, lo].astype(F32) + r1lo[half].astype(F32)).astype(BF16)
        e = put(part.at[half, t, lo], rl.at[half, lo], to_line(half, 1))
        got(b, r1hi.at[half])
        t = plus(me, 3)
        part[half, t, hi] = (part[half, t, hi].astype(F32) + r1hi[half].astype(F32)).astype(BF16)
        f = put(part.at[half, t, hi], rr.at[half, hi], to_line(half, 3))
        k_rs2.append((e, f))

    def mixed_terms(hs, acc):
        for xs in range(4):
            rows = jnp.concatenate([xa[hs, xs, ys].reshape(128, 128) for ys in range(4)], axis=1)
            s0 = (xs * 2 + hs) * 4
            cols = jnp.concatenate(
                [
                    wo[pl.ds(s0, 4)].reshape(512, 128),
                    wp[pl.ds(s0, 4)].reshape(512, 128),
                ],
                axis=1,
            )
            acc = acc + jnp.dot(rows, cols, preferred_element_type=F32)
        return acc

    ag2_wait(x_own, 4, own3)
    acc = mixed_terms(h, jnp.zeros((128, 256), F32))
    mixp[...] = acc

    got(k_zx, xa.at[oh, x, y])
    other1 = ag1(x_other, 4)

    for s in range(8):
        got(z_recv + s, xb.at[x, y, s])
    block1 = ag1(x_block, 8)

    k_s2 = []
    for half in (0, 1):
        me, me2 = (x, y) if half == 0 else (y, x)
        got(k_rs[half][2], rl.at[half, hi])
        got(k_rs[half][3], rr.at[half, lo])
        got(k_rs2[half][0], rl.at[half, lo])
        got(k_rs2[half][1], rr.at[half, hi])
        total = part[half, me].astype(F32) + rl[half].astype(F32) + rr[half].astype(F32)
        s1[half] = total
        b2[half] = total.astype(BF16)
        ks = []
        for j in (1, 3, 2):
            t = plus(me2, j)
            ks.append((j, put(b2.at[half, t], r2.at[half, j - 1], to_line2(half, j))))
        k_s2.append(ks)

    ag1_wait(x_other, 4, other1)
    other2 = ag2(x_other, 4)
    ag1_wait(x_block, 8, block1)
    block2 = ag2(x_block, 8)

    for half in (0, 1):
        me2 = y if half == 0 else x
        for j, k in k_s2[half]:
            got(k, r2.at[half, j - 1])
        tt[half] = (
            s1[half, me2]
            + r2[half, 0].astype(F32)
            + r2[half, 1].astype(F32)
            + r2[half, 2].astype(F32)
        )
    zs[...] = tt[:, oh].astype(BF16)
    k_zr = put(zs, zr, dev(h_=oh))

    other3 = ag2_forward(x_other, 4, other2)
    block3 = ag2_forward(x_block, 8, block2)

    for j, kd, kb in k_do:
        s = lax.rem(d + 8 - j, 8)
        got(kd, do.at[:, s])
        got(kb, bs.at[s])
    k_dp = put(do, dp_, dev(c_=oc))

    ag2_wait(x_other, 4, other3)
    acc = mixed_terms(oh, mixp[...])
    mixp[...] = acc
    k_mix = put(mixp.at[:, pl.ds(128, 128)], mixr, dev(c_=oc))

    ag2_wait(x_block, 8, block3)
    got(k_dp, dp_)
    tn = (((0,), (0,)), ((), ()))
    acc = jnp.zeros((512, 256), F32)
    for xs in range(4):
        feats = jnp.concatenate([xb[xs, ys].reshape(256, 128) for ys in range(4)], axis=1)
        cols = jnp.concatenate([do[xs].reshape(256, 128), dp_[xs].reshape(256, 128)], axis=1)
        acc = acc + lax.dot_general(feats, cols, tn, preferred_element_type=F32)
    acc = acc * scale
    gws[...] = acc[:, 128:256].reshape(4, 128, 128)
    k_gw = put(gws, gw.at[:, c], dev(c_=oc))
    gw[:, c] = acc[:, 0:128].reshape(4, 128, 128)

    gbias[...] = jnp.sum(bs[:, 0], axis=0, keepdims=True) * scale

    got(k_mix, mixr)
    mixed = mixp[:, 0:128] + mixr[...] + bias[...]
    crossed[...] = (basef * mixed + lay[...].reshape(128, 128).astype(F32)).astype(BF16)
    gbase[...] = (upper * mixed).astype(BF16)

    got(k_zr, zr)
    back = (tt[:, h] + zr[...].astype(F32)).reshape(128, 128)
    glayer[...] = (upper + back.T).astype(BF16)

    got(k_gw, gw.at[:, oc])
    for copy in sent:
        copy.wait_send()
    for mine, copy in z_sent:

        @pl.when(jnp.logical_not(mine))
        def _(copy=copy):
            copy.wait_send()


def local(base_rows, layer_rows, cross_weight, cross_bias, upstream):
    vmem = pl.BlockSpec(memory_space=pltpu.VMEM)
    scale = float((base_rows.shape[0] * 8) ** -0.5)
    small = jax.ShapeDtypeStruct((128, 128), BF16)
    crossed, gbase, glayer, gw, gbias = pl.pallas_call(
        functools.partial(kernel, scale),
        out_shape=(
            small,
            small,
            small,
            jax.ShapeDtypeStruct((4, 2, 128, 128), F32),
            jax.ShapeDtypeStruct((1, 128), F32),
        ),
        in_specs=[vmem, vmem, vmem, vmem, pl.BlockSpec(memory_space=pl.ANY)],
        out_specs=(vmem, vmem, vmem, vmem, vmem),
        scratch_shapes=[
            pltpu.VMEM((32, 128, 128), BF16),
            pltpu.VMEM((32, 128, 128), BF16),
            pltpu.VMEM((4, 32, 128), BF16),
            pltpu.VMEM((4, 32, 128), BF16),
            pltpu.VMEM((2, 4, 4, 4, 32, 128), BF16),
            pltpu.VMEM((4, 32, 128), BF16),
            pltpu.VMEM((4, 4, 8, 32, 128), BF16),
            pltpu.VMEM((4, 8, 32, 128), BF16),
            pltpu.VMEM((4, 8, 32, 128), BF16),
            pltpu.VMEM((8, 8, 128), F32),
            pltpu.VMEM((2, 4, 4, 2, 64, 128), BF16),
            pltpu.VMEM((2, 2, 2, 64, 128), BF16),
            pltpu.VMEM((2, 2, 2, 64, 128), BF16),
            pltpu.VMEM((2, 4, 2, 64, 128), BF16),
            pltpu.VMEM((2, 4, 2, 64, 128), BF16),
            pltpu.VMEM((2, 4, 2, 64, 128), F32),
            pltpu.VMEM((2, 4, 2, 64, 128), BF16),
            pltpu.VMEM((2, 3, 2, 64, 128), BF16),
            pltpu.VMEM((2, 2, 64, 128), F32),
            pltpu.VMEM((2, 64, 128), BF16),
            pltpu.VMEM((2, 64, 128), BF16),
            pltpu.VMEM((128, 256), F32),
            pltpu.VMEM((128, 128), F32),
            pltpu.VMEM((4, 128, 128), F32),
            pltpu.SemaphoreType.DMA((N_SEMS,)),
            pltpu.SemaphoreType.DMA((N_SEMS,)),
            pltpu.SemaphoreType.DMA((2,)),
        ],
        compiler_params=pltpu.CompilerParams(collective_id=0, has_side_effects=True),
        name="cross_layer",
    )(
        base_rows,
        layer_rows.reshape(4, 32, 128),
        upstream,
        cross_bias.reshape(1, 128),
        cross_weight.reshape(32, 2, 128, 128),
    )
    return crossed, gbase, glayer, gw.reshape(1024, 128), gbias.reshape(128)


def solution(mesh):
    return jax.shard_map(
        local,
        mesh=mesh,
        in_specs=(P("dp", "mp"), P("dp", "mp"), P(None, "mp"), P("mp"), P("dp", "mp")),
        out_specs=(P("dp", "mp"), P("dp", "mp"), P("dp", "mp"), P("dp", "mp"), P("mp")),
        check_vma=False,
    )
```

```python
import functools

import jax
import jax.numpy as jnp
from jax import lax
from jax.experimental import pallas as pl
from jax.experimental.pallas import tpu as pltpu
from jax.sharding import PartitionSpec as P

MESH = pl.DeviceIdType.MESH
F32 = jnp.float32
BF16 = jnp.bfloat16
N_SEMS = 128


def kernel(
    scale,
    base_hbm,
    lay_hbm,
    up_hbm,
    bias_hbm,
    w4,
    crossed,
    gbase,
    glayer,
    gw,
    gbias,
    base,
    lay,
    up,
    bias,
    wo,
    wp,
    dl,
    dlp,
    xa,
    fs,
    xb,
    do,
    dp_,
    bs,
    part,
    r1lo,
    r1hi,
    rl,
    rr,
    s1,
    b2,
    r2,
    tt,
    zs,
    zr,
    mixp,
    mixr,
    gws,
    send,
    recv,
    lsem,
):
    d = lax.axis_index("dp")
    m = lax.axis_index("mp")
    c = lax.rem(m, 2)
    y = lax.rem(lax.div(m, 2), 4)
    h = lax.rem(lax.div(m, 8), 2)
    x = lax.div(m, 16)
    oh = 1 - h
    oc = 1 - c

    def dev(x_=None, y_=None, h_=None, c_=None, d_=None):
        x_ = x if x_ is None else x_
        y_ = y if y_ is None else y_
        h_ = h if h_ is None else h_
        c_ = c if c_ is None else c_
        d_ = d if d_ is None else d_
        return (d_, ((x_ * 2 + h_) * 4 + y_) * 2 + c_)

    def plus(v, k):
        return lax.rem(v + k, 4)

    ids = iter(range(N_SEMS))
    sent = []

    def put(src, dst, to, k=None):
        k = next(ids) if k is None else k
        copy = pltpu.make_async_remote_copy(
            src_ref=src,
            dst_ref=dst,
            send_sem=send.at[k],
            recv_sem=recv.at[k],
            device_id=to,
            device_id_type=MESH,
        )
        copy.start()
        sent.append(copy)
        return k

    def got(k, landed):
        pltpu.make_async_remote_copy(
            src_ref=landed,
            dst_ref=landed,
            send_sem=send.at[k],
            recv_sem=recv.at[k],
            device_id=dev(c_=oc),
            device_id_type=MESH,
        ).wait_recv()

    barrier = pltpu.get_barrier_semaphore()
    near = [dev(c_=oc)]
    near += [dev(x_=plus(x, k)) for k in (1, 2, 3)]
    near += [dev(y_=plus(y, k)) for k in (1, 2, 3)]
    z = h * 8 + d
    for k in range(1, 16):
        zk = lax.rem(z + k, 16)
        near.append(dev(h_=lax.div(zk, 8), d_=lax.rem(zk, 8)))
    for to in near:
        pl.semaphore_signal(barrier, inc=1, device_id=to, device_id_type=MESH)

    loads = [
        pltpu.make_async_copy(src, dst, lsem.at[k])
        for k, (src, dst) in enumerate(
            (
                (up_hbm, up),
                (base_hbm, base),
                (lay_hbm, lay),
                (lay_hbm, xa.at[h, x, y]),
                (bias_hbm, bias),
                (w4.at[:, c], wo),
            )
        )
    ]
    for load in loads:
        load.start()
    loads[0].wait()
    loads[1].wait()

    upper = up[...].astype(F32)
    basef = base[...].astype(F32)
    delta = upper * basef
    low = delta.astype(BF16).reshape(4, 32, 128)
    dl[...] = low
    do[:, d] = low
    bs[d] = jnp.broadcast_to(jnp.sum(delta, axis=0, keepdims=True), (8, 128))

    loads[2].wait()
    loads[3].wait()
    pl.semaphore_wait(barrier, len(near))

    k_dlp = put(dl, dlp, dev(c_=oc))
    k_wp = [
        put(w4.at[pl.ds(8 * j, 8), oc], wp.at[pl.ds(8 * j, 8)], dev(c_=oc))
        for j in range(4)
    ]
    k_zx = put(lay, xa.at[h, x, y], dev(h_=oh))

    def ag1(view, n):
        half = n // 2
        ks = []
        for j in (1, 3, 2):
            a = view(x, y, 0, half)
            b = view(x, y, half, half)
            ka = put(a, a, dev(x_=plus(x, j)))
            kb = put(b, b, dev(y_=plus(y, j)))
            ks.append((j, ka, kb))
        return ks

    def ag1_wait(view, n, ks):
        half = n // 2
        for j, ka, kb in ks:
            got(ka, view(plus(x, 4 - j), y, 0, half))
            got(kb, view(x, plus(y, 4 - j), half, half))

    every = pl.ds(0, 4)

    def ag2(view, n):
        half = n // 2
        ks = []
        for j in (1, 3):
            a = view(every, y, 0, half)
            b = view(x, every, half, half)
            ks.append((put(a, a, dev(y_=plus(y, j))), put(b, b, dev(x_=plus(x, j)))))
        return ks

    def ag2_forward(view, n, ks):
        half = n // 2
        out = []
        for (ka, kb), j, part_of in zip(ks, (1, 3), (pl.ds(0, 2), pl.ds(2, 2)), strict=True):
            ys, xs = plus(y, 4 - j), plus(x, 4 - j)
            got(ka, view(every, ys, 0, half))
            a = view(part_of, ys, 0, half)
            fa = put(a, a, dev(y_=plus(y, j)))
            got(kb, view(xs, every, half, half))
            b = view(xs, part_of, half, half)
            fb = put(b, b, dev(x_=plus(x, j)))
            out.append((fa, fb, part_of))
        return out

    def ag2_wait(view, n, ks):
        half = n // 2
        for fa, fb, part_of in ks:
            got(fa, view(part_of, plus(y, 2), 0, half))
            got(fb, view(plus(x, 2), part_of, half, half))

    def x_own(xs, ys, q, nq):
        return xa.at[h, xs, ys, pl.ds(q, nq)]

    def x_other(xs, ys, q, nq):
        return xa.at[oh, xs, ys, pl.ds(q, nq)]

    def x_block(xs, ys, q, nq):
        return xb.at[xs, ys, pl.ds(q, nq)]

    own1 = ag1(x_own, 4)

    k_fs = []
    for j in (1, 2, 3):
        t = plus(x, j)
        k_fs.append(put(lay.at[t], fs.at[x], dev(x_=t)))
    for j, k in zip((1, 2, 3), k_fs, strict=True):
        got(k, fs.at[plus(x, 4 - j)])
    z_first = [next(ids) for _ in range(8)]
    z_recv = z_first[0]
    z_sent = []
    for j in range(4):
        for hh in (0, 1):
            s = plus(x, j)
            src = lay.at[x] if j == 0 else fs.at[s]
            d_to = 2 * s + h
            mine = jnp.logical_and(h == hh, d_to == d)
            dst = xb.at[x, y, d]
            copy = pltpu.make_async_remote_copy(
                src_ref=src,
                dst_ref=dst,
                send_sem=send.at[z_first[2 * j + hh]],
                recv_sem=recv.at[z_recv + d],
                device_id=dev(h_=hh, d_=d_to),
                device_id_type=MESH,
            )
            stay = pltpu.make_async_copy(src, dst, recv.at[z_recv + d])

            @pl.when(mine)
            def _(stay=stay):
                stay.start()

            @pl.when(jnp.logical_not(mine))
            def _(copy=copy):
                copy.start()

            z_sent.append((mine, copy))

    k_do = []
    for j in range(1, 8):
        t = lax.rem(d + j, 8)
        kd = put(dl, do.at[:, d], dev(d_=t))
        kb = put(bs.at[d], bs.at[d], dev(d_=t))
        k_do.append((j, kd, kb))

    ag1_wait(x_own, 4, own1)
    own2 = ag2(x_own, 4)

    loads[5].wait()
    got(k_dlp, dlp)
    d_own = dl[...].reshape(128, 128)
    d_other = dlp[...].reshape(128, 128)
    nt = (((1,), (1,)), ((), ()))
    for i in range(8):
        if i % 2 == 0:
            got(k_wp[i // 2], wp.at[pl.ds(4 * i, 8)])
        xs, hs = i // 2, i % 2
        term = lax.dot_general(
            wo[4 * i : 4 * i + 4].reshape(512, 128), d_own, nt, preferred_element_type=F32
        ) + lax.dot_general(
            wp[4 * i : 4 * i + 4].reshape(512, 128), d_other, nt, preferred_element_type=F32
        )
        term = term.astype(BF16).reshape(4, 128, 128)
        part[0, xs, :, hs] = term[:, 0:64]
        for ys in range(4):
            part[1, ys, xs, hs] = term[ys, 64:128]

    lo, hi = pl.ds(0, 2), pl.ds(2, 2)

    def to_line(half, j):
        return dev(x_=plus(x, j)) if half == 0 else dev(y_=plus(y, j))

    def to_line2(half, j):
        return dev(y_=plus(y, j)) if half == 0 else dev(x_=plus(x, j))

    k_rs = []
    for half in (0, 1):
        me = x if half == 0 else y
        a = put(part.at[half, plus(me, 2), lo], r1lo.at[half], to_line(half, 1))
        b = put(part.at[half, plus(me, 2), hi], r1hi.at[half], to_line(half, 3))
        e = put(part.at[half, plus(me, 1), hi], rl.at[half, hi], to_line(half, 1))
        f = put(part.at[half, plus(me, 3), lo], rr.at[half, lo], to_line(half, 3))
        k_rs.append((a, b, e, f))

    own3 = ag2_forward(x_own, 4, own2)

    k_rs2 = []
    for half in (0, 1):
        me = x if half == 0 else y
        a, b, _, _ = k_rs[half]
        got(a, r1lo.at[half])
        t = plus(me, 1)
        part[half, t, lo] = (part[half, t, lo].astype(F32) + r1lo[half].astype(F32)).astype(BF16)
        e = put(part.at[half, t, lo], rl.at[half, lo], to_line(half, 1))
        got(b, r1hi.at[half])
        t = plus(me, 3)
        part[half, t, hi] = (part[half, t, hi].astype(F32) + r1hi[half].astype(F32)).astype(BF16)
        f = put(part.at[half, t, hi], rr.at[half, hi], to_line(half, 3))
        k_rs2.append((e, f))

    def mixed_terms(hs, acc):
        for xs in range(4):
            rows = jnp.concatenate([xa[hs, xs, ys].reshape(128, 128) for ys in range(4)], axis=1)
            s0 = (xs * 2 + hs) * 4
            cols = jnp.concatenate(
                [
                    wo[pl.ds(s0, 4)].reshape(512, 128),
                    wp[pl.ds(s0, 4)].reshape(512, 128),
                ],
                axis=1,
            )
            acc = acc + jnp.dot(rows, cols, preferred_element_type=F32)
        return acc

    ag2_wait(x_own, 4, own3)
    acc = mixed_terms(h, jnp.zeros((128, 256), F32))
    mixp[...] = acc

    got(k_zx, xa.at[oh, x, y])
    other1 = ag1(x_other, 4)

    for s in range(8):
        got(z_recv + s, xb.at[x, y, s])
    block1 = ag1(x_block, 8)

    k_s2 = []
    for half in (0, 1):
        me, me2 = (x, y) if half == 0 else (y, x)
        got(k_rs[half][2], rl.at[half, hi])
        got(k_rs[half][3], rr.at[half, lo])
        got(k_rs2[half][0], rl.at[half, lo])
        got(k_rs2[half][1], rr.at[half, hi])
        total = part[half, me].astype(F32) + rl[half].astype(F32) + rr[half].astype(F32)
        s1[half] = total
        b2[half] = total.astype(BF16)
        ks = []
        for j in (1, 3, 2):
            t = plus(me2, j)
            ks.append((j, put(b2.at[half, t], r2.at[half, j - 1], to_line2(half, j))))
        k_s2.append(ks)

    ag1_wait(x_other, 4, other1)
    other2 = ag2(x_other, 4)
    ag1_wait(x_block, 8, block1)
    block2 = ag2(x_block, 8)

    for half in (0, 1):
        me2 = y if half == 0 else x
        for j, k in k_s2[half]:
            got(k, r2.at[half, j - 1])
        tt[half] = (
            s1[half, me2]
            + r2[half, 0].astype(F32)
            + r2[half, 1].astype(F32)
            + r2[half, 2].astype(F32)
        )
    zs[...] = tt[:, oh].astype(BF16)
    k_zr = put(zs, zr, dev(h_=oh))

    other3 = ag2_forward(x_other, 4, other2)
    block3 = ag2_forward(x_block, 8, block2)

    for j, kd, kb in k_do:
        s = lax.rem(d + 8 - j, 8)
        got(kd, do.at[:, s])
        got(kb, bs.at[s])
    k_dp = put(do, dp_, dev(c_=oc))

    ag2_wait(x_other, 4, other3)
    acc = mixed_terms(oh, mixp[...])
    mixp[...] = acc
    k_mix = put(mixp.at[:, pl.ds(128, 128)], mixr, dev(c_=oc))

    ag2_wait(x_block, 8, block3)
    got(k_dp, dp_)
    tn = (((0,), (0,)), ((), ()))
    acc = jnp.zeros((512, 256), F32)
    for xs in range(4):
        feats = jnp.concatenate([xb[xs, ys].reshape(256, 128) for ys in range(4)], axis=1)
        cols = jnp.concatenate([do[xs].reshape(256, 128), dp_[xs].reshape(256, 128)], axis=1)
        acc = acc + lax.dot_general(feats, cols, tn, preferred_element_type=F32)
    acc = acc * scale
    gws[...] = acc[:, 128:256].reshape(4, 128, 128)
    k_gw = put(gws, gw.at[:, c], dev(c_=oc))
    gw[:, c] = acc[:, 0:128].reshape(4, 128, 128)

    gbias[...] = jnp.sum(bs[:, 0], axis=0, keepdims=True) * scale

    got(k_mix, mixr)
    loads[4].wait()
    mixed = mixp[:, 0:128] + mixr[...] + bias[...]
    crossed[...] = (basef * mixed + lay[...].reshape(128, 128).astype(F32)).astype(BF16)
    gbase[...] = (upper * mixed).astype(BF16)

    got(k_zr, zr)
    back = (tt[:, h] + zr[...].astype(F32)).reshape(128, 128)
    glayer[...] = (upper + back.T).astype(BF16)

    got(k_gw, gw.at[:, oc])
    for copy in sent:
        copy.wait_send()
    for mine, copy in z_sent:

        @pl.when(jnp.logical_not(mine))
        def _(copy=copy):
            copy.wait_send()


def finish(a, b, e, g, s, oa, ob, oe, og, os_, sem):
    copies = [
        pltpu.make_async_copy(src, dst, sem.at[k])
        for k, (src, dst) in enumerate(((g, og), (a, oa), (b, ob), (e, oe), (s, os_)))
    ]
    for copy in copies:
        copy.start()
    for copy in copies:
        copy.wait()


def local(base_rows, layer_rows, cross_weight, cross_bias, upstream):
    vmem = pl.BlockSpec(memory_space=pltpu.VMEM)
    hbm = pl.BlockSpec(memory_space=pltpu.HBM)
    scale = float((base_rows.shape[0] * 8) ** -0.5)
    small = jax.ShapeDtypeStruct((128, 128), BF16)
    shapes = (
        small,
        small,
        small,
        jax.ShapeDtypeStruct((4, 2, 128, 128), F32),
        jax.ShapeDtypeStruct((1, 128), F32),
    )
    results = pl.pallas_call(
        functools.partial(kernel, scale),
        out_shape=shapes,
        in_specs=[hbm] * 5,
        out_specs=(vmem, vmem, vmem, vmem, vmem),
        scratch_shapes=[
            pltpu.VMEM((128, 128), BF16),
            pltpu.VMEM((4, 32, 128), BF16),
            pltpu.VMEM((128, 128), BF16),
            pltpu.VMEM((1, 128), F32),
            pltpu.VMEM((32, 128, 128), BF16),
            pltpu.VMEM((32, 128, 128), BF16),
            pltpu.VMEM((4, 32, 128), BF16),
            pltpu.VMEM((4, 32, 128), BF16),
            pltpu.VMEM((2, 4, 4, 4, 32, 128), BF16),
            pltpu.VMEM((4, 32, 128), BF16),
            pltpu.VMEM((4, 4, 8, 32, 128), BF16),
            pltpu.VMEM((4, 8, 32, 128), BF16),
            pltpu.VMEM((4, 8, 32, 128), BF16),
            pltpu.VMEM((8, 8, 128), F32),
            pltpu.VMEM((2, 4, 4, 2, 64, 128), BF16),
            pltpu.VMEM((2, 2, 2, 64, 128), BF16),
            pltpu.VMEM((2, 2, 2, 64, 128), BF16),
            pltpu.VMEM((2, 4, 2, 64, 128), BF16),
            pltpu.VMEM((2, 4, 2, 64, 128), BF16),
            pltpu.VMEM((2, 4, 2, 64, 128), F32),
            pltpu.VMEM((2, 4, 2, 64, 128), BF16),
            pltpu.VMEM((2, 3, 2, 64, 128), BF16),
            pltpu.VMEM((2, 2, 64, 128), F32),
            pltpu.VMEM((2, 64, 128), BF16),
            pltpu.VMEM((2, 64, 128), BF16),
            pltpu.VMEM((128, 256), F32),
            pltpu.VMEM((128, 128), F32),
            pltpu.VMEM((4, 128, 128), F32),
            pltpu.SemaphoreType.DMA((N_SEMS,)),
            pltpu.SemaphoreType.DMA((N_SEMS,)),
            pltpu.SemaphoreType.DMA((6,)),
        ],
        compiler_params=pltpu.CompilerParams(
            collective_id=0, has_side_effects=True, vmem_limit_bytes=24 << 20
        ),
        name="cross_layer",
    )(
        *(
            pltpu.with_memory_space_constraint(a, pltpu.HBM)
            for a in (
                base_rows,
                layer_rows.reshape(4, 32, 128),
                upstream,
                cross_bias.reshape(1, 128),
                cross_weight.reshape(32, 2, 128, 128),
            )
        )
    )
    crossed, gbase, glayer, gw, gbias = pl.pallas_call(
        finish,
        out_shape=shapes,
        in_specs=[vmem] * 5,
        out_specs=(pl.BlockSpec(memory_space=pl.ANY),) * 5,
        scratch_shapes=[pltpu.SemaphoreType.DMA((5,))],
        compiler_params=pltpu.CompilerParams(vmem_limit_bytes=4 << 20),
        name="finish",
    )(*results)
    return crossed, gbase, glayer, gw.reshape(1024, 128), gbias.reshape(128)


def solution(mesh):
    return jax.shard_map(
        local,
        mesh=mesh,
        in_specs=(P("dp", "mp"), P("dp", "mp"), P(None, "mp"), P("mp"), P("dp", "mp")),
        out_specs=(P("dp", "mp"), P("dp", "mp"), P("dp", "mp"), P("dp", "mp"), P("mp")),
        check_vma=False,
    )
```

```python
import functools
import math

import jax
import jax.numpy as jnp
from jax import lax
from jax.experimental import pallas as pl
from jax.experimental.pallas import tpu as pltpu
from jax.sharding import PartitionSpec as P

MESH = pl.DeviceIdType.MESH
F32 = jnp.float32
BF16 = jnp.bfloat16
N_SENDS = 14
N_RECVS = 49
MOST_ROWS = 4096


def kernel(
    scale,
    base_hbm,
    lay_hbm,
    up_hbm,
    bias_hbm,
    w4,
    crossed,
    gbase,
    glayer,
    gw,
    gbias,
    base,
    lay,
    up,
    bias,
    wo,
    wp,
    dl,
    dlp,
    xa,
    xb,
    do,
    dp_,
    bs,
    part,
    r1lo,
    r1hi,
    rl,
    rr,
    s1,
    b2s,
    r2,
    tt,
    zs,
    zr,
    mixp,
    mixr,
    gws,
    tally,
    send,
    recv,
    lsem,
):
    d = lax.axis_index("dp")
    m = lax.axis_index("mp")
    c = lax.rem(m, 2)
    y = lax.rem(lax.div(m, 2), 4)
    h = lax.rem(lax.div(m, 8), 2)
    x = lax.div(m, 16)
    oh = 1 - h
    oc = 1 - c

    def dev(x_=None, y_=None, h_=None, c_=None, d_=None):
        x_ = x if x_ is None else x_
        y_ = y if y_ is None else y_
        h_ = h if h_ is None else h_
        c_ = c if c_ is None else c_
        d_ = d if d_ is None else d_
        return (d_, ((x_ * 2 + h_) * 4 + y_) * 2 + c_)

    def plus(v, k):
        return lax.rem(v + k, 4)

    ids = iter(range(N_RECVS))
    send_ids = iter(range(N_SENDS))
    sent = [[next(send_ids), 0]]

    def rows(ref):
        return math.prod(ref.shape) * jnp.dtype(ref.dtype).itemsize // 256

    def wait_rows(sem, n):
        view = tally.at[pl.ds(0, n)]
        pltpu.make_async_copy(view, view, sem).wait()

    def put(src, dst, to, k=None):
        k = next(ids) if k is None else k
        n = rows(src)
        if sent[-1][1] + n > MOST_ROWS:
            sent.append([next(send_ids), 0])
        sent[-1][1] += n
        pltpu.make_async_remote_copy(
            src_ref=src,
            dst_ref=dst,
            send_sem=send.at[sent[-1][0]],
            recv_sem=recv.at[k],
            device_id=to,
            device_id_type=MESH,
        ).start()
        return k

    def got(k, *landed):
        wait_rows(recv.at[k], sum(rows(ref) for ref in landed))

    b4, b2, b1 = lax.div(d, 4), lax.rem(lax.div(d, 2), 2), lax.rem(d, 2)
    mine = d == 2 * x + h

    def first_row(d_, h_):
        window = jnp.clip(d_ - 2, 0, 4)
        return jnp.where(lax.rem(d_, 2) == h_, window, window + 4)

    barrier = pltpu.get_barrier_semaphore()
    near = [dev(c_=oc)]
    near += [dev(x_=plus(x, k)) for k in (1, 2, 3)]
    near += [dev(y_=plus(y, k)) for k in (1, 2, 3)]
    near += [dev(h_=oh), dev(d_=d + 4 - 8 * b4), dev(d_=d + 2 - 4 * b2), dev(d_=d + 1 - 2 * b1)]
    for to in near:
        pl.semaphore_signal(barrier, inc=1, device_id=to, device_id_type=MESH)
    z_to = []
    for t in range(4):
        for hh in (0, 1):
            same = jnp.logical_and(x == t, jnp.logical_and(h == hh, mine))
            z_to.append((t, hh, same, dev(x_=t, h_=hh, d_=2 * x + h)))
    z_from = []
    for s in range(8):
        same = jnp.logical_and(d == s, mine)
        z_from.append((same, dev(x_=lax.div(d, 2), h_=lax.rem(d, 2), d_=s)))
    for same, to in [(same, to) for _, _, same, to in z_to] + z_from:

        @pl.when(jnp.logical_not(same))
        def _(to=to):
            pl.semaphore_signal(barrier, inc=1, device_id=to, device_id_type=MESH)

    n_signals = len(near) + 16 - 2 * mine.astype(jnp.int32)

    loads = [
        pltpu.make_async_copy(src, dst, lsem.at[k])
        for k, (src, dst) in enumerate(
            (
                (lay_hbm, lay),
                (up_hbm, up),
                (base_hbm, base),
                (lay_hbm, xa.at[h, x, y]),
                (bias_hbm, bias),
                (w4.at[:, :, :, c], wo),
            )
        )
    ]
    for load in loads:
        load.start()
    loads[0].wait()
    pl.semaphore_wait(barrier, n_signals)

    def ag1(view, n):
        half = n // 2
        k = next(ids)
        for j in (1, 3, 2):
            a = view(x, y, 0, half)
            b = view(x, y, half, half)
            put(a, a, dev(x_=plus(x, j)), k)
            put(b, b, dev(y_=plus(y, j)), k)
        return k

    def ag1_wait(view, n, k):
        half = n // 2
        got(k, *[view(x, y, 0, half)] * 3, *[view(x, y, half, half)] * 3)

    every = pl.ds(0, 4)

    def ag2(view, n):
        half = n // 2
        ks = []
        for j in (1, 3):
            a = view(every, y, 0, half)
            b = view(x, every, half, half)
            ks.append((put(a, a, dev(y_=plus(y, j))), put(b, b, dev(x_=plus(x, j)))))
        return ks

    def ag2_forward(view, n, ks):
        half = n // 2
        k = next(ids)
        for (ka, kb), j, part_of in zip(ks, (1, 3), (pl.ds(0, 2), pl.ds(2, 2)), strict=True):
            ys, xs = plus(y, 4 - j), plus(x, 4 - j)
            got(ka, view(every, ys, 0, half))
            a = view(part_of, ys, 0, half)
            put(a, a, dev(y_=plus(y, j)), k)
            got(kb, view(xs, every, half, half))
            b = view(xs, part_of, half, half)
            put(b, b, dev(x_=plus(x, j)), k)
        return k

    def ag2_wait(view, n, k):
        half = n // 2
        got(k, view(every, y, 0, half), view(x, every, half, half))

    def x_own(xs, ys, q, nq):
        return xa.at[h, xs, ys, pl.ds(q, nq)]

    def x_other(xs, ys, q, nq):
        return xa.at[oh, xs, ys, pl.ds(q, nq)]

    def x_block0(xs, ys, q, nq):
        return xb.at[xs, ys, pl.ds(q, nq)]

    def x_block1(xs, ys, q, nq):
        return xb.at[xs, ys, pl.ds(4 + q, nq)]

    z_first = [next(send_ids) for _ in range(8)]
    z_recv = next(ids)
    next(ids)
    z_sent = []
    for n, (t, hh, same, to) in enumerate(z_to):
        d_to = 2 * x + h
        slot = lax.rem(d + 8 - first_row(d_to, hh), 8)
        src, dst = lay.at[t], xb.at[t, y, slot]
        copy = pltpu.make_async_remote_copy(
            src_ref=src,
            dst_ref=dst,
            send_sem=send.at[z_first[n]],
            recv_sem=recv.at[z_recv + lax.div(slot, 4)],
            device_id=to,
            device_id_type=MESH,
        )
        stay = pltpu.make_async_copy(src, dst, recv.at[z_recv + lax.div(slot, 4)])

        @pl.when(same)
        def _(stay=stay):
            stay.start()

        @pl.when(jnp.logical_not(same))
        def _(copy=copy):
            copy.start()

        z_sent.append((same, copy))

    k_zx = put(lay, xa.at[h, x, y], dev(h_=oh))
    k_wp = [put(w4.at[:, oh, :, oc], wp.at[:, oh], dev(c_=oc))]
    loads[3].wait()
    own1 = ag1(x_own, 4)

    loads[1].wait()
    loads[2].wait()
    upper = up[...].astype(F32)
    basef = base[...].astype(F32)
    delta = upper * basef
    low = delta.astype(BF16).reshape(4, 32, 128)
    dl[...] = low
    do[:, b4, b2, b1] = low
    bs[b4, b2, b1] = jnp.broadcast_to(jnp.sum(delta, axis=0, keepdims=True), (8, 128))
    k_dlp = put(dl, dlp, dev(c_=oc))
    k_wp.append(put(w4.at[:, h, :, oc], wp.at[:, h], dev(c_=oc)))

    every2 = pl.ds(0, 2)
    steps = (
        (dev(d_=d + 4 - 8 * b4), (b4, b2, b1), (1 - b4, b2, b1)),
        (dev(d_=d + 2 - 4 * b2), (every2, b2, b1), (every2, 1 - b2, b1)),
        (dev(d_=d + 1 - 2 * b1), (every2, every2, b1), (every2, every2, 1 - b1)),
    )

    def along_z(step):
        to, here, _ = steps[step]
        a, b = do.at[(slice(None), *here)], bs.at[here]
        return put(b, b, to, put(a, a, to))

    def along_z_wait(step, k):
        theirs = steps[step][2]
        got(k, do.at[(slice(None), *theirs)], bs.at[theirs])

    k_d = along_z(0)

    loads[5].wait()
    got(k_dlp, dlp)
    d_own = dl[...].reshape(128, 128)
    d_other = dlp[...].reshape(128, 128)
    nt = (((1,), (1,)), ((), ()))
    lo, hi = pl.ds(0, 2), pl.ds(2, 2)

    def to_line(half, j):
        return dev(x_=plus(x, j)) if half == 0 else dev(y_=plus(y, j))

    def to_line2(half, j):
        return dev(y_=plus(y, j)) if half == 0 else dev(x_=plus(x, j))

    def back_terms(hs):
        for xs in range(4):
            term = lax.dot_general(
                wo[xs, hs].reshape(512, 128), d_own, nt, preferred_element_type=F32
            ) + lax.dot_general(
                wp[xs, hs].reshape(512, 128), d_other, nt, preferred_element_type=F32
            )
            term = term.astype(BF16).reshape(4, 128, 128)
            part[hs, 0, xs] = term[:, 0:64]
            for ys in range(4):
                part[hs, 1, ys, xs] = term[ys, 64:128]

    def rs1(hs):
        first, rest = [], next(ids)
        for half in (0, 1):
            me = x if half == 0 else y
            a = put(part.at[hs, half, plus(me, 2), lo], r1lo.at[hs, half], to_line(half, 1))
            b = put(part.at[hs, half, plus(me, 2), hi], r1hi.at[hs, half], to_line(half, 3))
            first.append((a, b))
        for half in (0, 1):
            me = x if half == 0 else y
            put(part.at[hs, half, plus(me, 1), hi], rl.at[hs, half, hi], to_line(half, 1), rest)
            put(part.at[hs, half, plus(me, 3), lo], rr.at[hs, half, lo], to_line(half, 3), rest)
        return first, rest

    def rs2(hs, ks):
        first, rest = ks
        for half in (0, 1):
            me = x if half == 0 else y
            a, b = first[half]
            got(a, r1lo.at[hs, half])
            t = plus(me, 1)
            part[hs, half, t, lo] = (
                part[hs, half, t, lo].astype(F32) + r1lo[hs, half].astype(F32)
            ).astype(BF16)
            put(part.at[hs, half, t, lo], rl.at[hs, half, lo], to_line(half, 1), rest)
            got(b, r1hi.at[hs, half])
            t = plus(me, 3)
            part[hs, half, t, hi] = (
                part[hs, half, t, hi].astype(F32) + r1hi[hs, half].astype(F32)
            ).astype(BF16)
            put(part.at[hs, half, t, hi], rr.at[hs, half, hi], to_line(half, 3), rest)
        return rest

    def rs3(hs, rest):
        got(rest, rl.at[hs], rr.at[hs])
        k = next(ids)
        for half in (0, 1):
            me, me2 = (x, y) if half == 0 else (y, x)
            total = (
                part[hs, half, me].astype(F32)
                + rl[hs, half].astype(F32)
                + rr[hs, half].astype(F32)
            )
            s1[hs, half] = total
            b2s[hs, half] = total.astype(BF16)
            for j in (1, 3, 2):
                t = plus(me2, j)
                put(b2s.at[hs, half, t], r2.at[hs, half, j - 1], to_line2(half, j), k)
        return k

    def rs4(hs, k):
        got(k, r2.at[hs])
        for half in (0, 1):
            me2 = y if half == 0 else x
            tt[hs, half] = (
                s1[hs, half, me2]
                + r2[hs, half, 0].astype(F32)
                + r2[hs, half, 1].astype(F32)
                + r2[hs, half, 2].astype(F32)
            )

    got(k_wp[0], wp.at[:, oh])
    back_terms(oh)
    k_far = rs1(oh)
    got(k_wp[1], wp.at[:, h])
    back_terms(h)
    k_near = rs1(h)

    ag1_wait(x_own, 4, own1)
    own2 = ag2(x_own, 4)
    k_far = rs2(oh, k_far)
    k_near = rs2(h, k_near)

    def mixed_terms(hs, acc):
        for xs in range(4):
            rows = jnp.concatenate([xa[hs, xs, ys].reshape(128, 128) for ys in range(4)], axis=1)
            cols = jnp.concatenate(
                [wo[xs, hs].reshape(512, 128), wp[xs, hs].reshape(512, 128)], axis=1
            )
            acc = acc + jnp.dot(rows, cols, preferred_element_type=F32)
        return acc

    quarter = xb.at[x, y, pl.ds(0, 4)]
    got(z_recv, quarter)
    first1 = ag1(x_block0, 4)
    got(k_zx, xa.at[oh, x, y])
    other1 = ag1(x_other, 4)
    k_far = rs3(oh, k_far)
    got(z_recv + 1, quarter)
    second1 = ag1(x_block1, 4)
    k_near = rs3(h, k_near)

    along_z_wait(0, k_d)
    k_d = along_z(1)
    own3 = ag2_forward(x_own, 4, own2)
    ag1_wait(x_block0, 4, first1)
    first2 = ag2(x_block0, 4)
    ag1_wait(x_other, 4, other1)
    other2 = ag2(x_other, 4)

    rs4(oh, k_far)
    zs[...] = tt[oh].astype(BF16)
    k_zr = put(zs, zr, dev(h_=oh))

    ag1_wait(x_block1, 4, second1)
    second2 = ag2(x_block1, 4)
    along_z_wait(1, k_d)
    k_d = along_z(2)
    ag2_wait(x_own, 4, own3)
    mixp[...] = mixed_terms(h, jnp.zeros((128, 256), F32))

    first3 = ag2_forward(x_block0, 4, first2)
    other3 = ag2_forward(x_other, 4, other2)
    rs4(h, k_near)
    second3 = ag2_forward(x_block1, 4, second2)
    along_z_wait(2, k_d)
    k_dp = put(do, dp_, dev(c_=oc))

    ag2_wait(x_other, 4, other3)
    mixp[...] = mixed_terms(oh, mixp[...])
    k_mix = put(mixp.at[:, pl.ds(128, 128)], mixr, dev(c_=oc))

    tn = (((0,), (0,)), ((), ()))

    def rows_of(ref, xs, g):
        out = []
        for k in range(4):
            s = lax.rem(first_row(d, h) + 4 * g + k, 8)
            out.append(ref[xs, lax.div(s, 4), lax.rem(lax.div(s, 2), 2), lax.rem(s, 2)])
        return jnp.concatenate(out, axis=0)

    def weight_terms(g):
        feats = jnp.concatenate(
            [
                jnp.concatenate(
                    [xb[xs, ys, 4 * g : 4 * g + 4].reshape(128, 128) for ys in range(4)], axis=1
                )
                for xs in range(4)
            ],
            axis=0,
        )
        cols = jnp.concatenate(
            [
                jnp.concatenate(
                    [rows_of(do, xs, g), rows_of(dp_, xs, g)], axis=1
                )
                for xs in range(4)
            ],
            axis=0,
        )
        return lax.dot_general(feats, cols, tn, preferred_element_type=F32)

    got(k_dp, dp_)
    ag2_wait(x_block0, 4, first3)
    acc = weight_terms(0)
    ag2_wait(x_block1, 4, second3)
    acc = acc + weight_terms(1)
    acc = acc * scale
    gws[...] = acc[:, 128:256].reshape(4, 128, 128)
    k_gw = put(gws, gw.at[:, c], dev(c_=oc))
    gw[:, c] = acc[:, 0:128].reshape(4, 128, 128)

    gbias[...] = jnp.sum(bs[...].reshape(8, 8, 128)[:, 0], axis=0, keepdims=True) * scale

    got(k_mix, mixr)
    loads[4].wait()
    mixed = mixp[:, 0:128] + mixr[...] + bias[...]
    crossed[...] = (basef * mixed + lay[...].reshape(128, 128).astype(F32)).astype(BF16)
    gbase[...] = (upper * mixed).astype(BF16)

    got(k_zr, zr)
    back = (tt[h] + zr[...].astype(F32)).reshape(128, 128)
    glayer[...] = (upper + back.T).astype(BF16)

    got(k_gw, gw.at[:, oc])
    for k, n in sent:
        wait_rows(send.at[k], n)
    for same, copy in z_sent:

        @pl.when(jnp.logical_not(same))
        def _(copy=copy):
            copy.wait_send()


def finish(a, b, e, g, s, oa, ob, oe, og, os_, sem):
    copies = [
        pltpu.make_async_copy(src, dst, sem.at[k])
        for k, (src, dst) in enumerate(((g, og), (a, oa), (b, ob), (e, oe), (s, os_)))
    ]
    for copy in copies:
        copy.start()
    for copy in copies:
        copy.wait()


def local(base_rows, layer_rows, cross_weight, cross_bias, upstream):
    vmem = pl.BlockSpec(memory_space=pltpu.VMEM)
    hbm = pl.BlockSpec(memory_space=pltpu.HBM)
    scale = float((base_rows.shape[0] * 8) ** -0.5)
    small = jax.ShapeDtypeStruct((128, 128), BF16)
    shapes = (
        small,
        small,
        small,
        jax.ShapeDtypeStruct((4, 2, 128, 128), F32),
        jax.ShapeDtypeStruct((1, 128), F32),
    )
    results = pl.pallas_call(
        functools.partial(kernel, scale),
        out_shape=shapes,
        in_specs=[hbm] * 5,
        out_specs=(vmem, vmem, vmem, vmem, vmem),
        scratch_shapes=[
            pltpu.VMEM((128, 128), BF16),
            pltpu.VMEM((4, 32, 128), BF16),
            pltpu.VMEM((128, 128), BF16),
            pltpu.VMEM((1, 128), F32),
            pltpu.VMEM((4, 2, 4, 128, 128), BF16),
            pltpu.VMEM((4, 2, 4, 128, 128), BF16),
            pltpu.VMEM((4, 32, 128), BF16),
            pltpu.VMEM((4, 32, 128), BF16),
            pltpu.VMEM((2, 4, 4, 4, 32, 128), BF16),
            pltpu.VMEM((4, 4, 8, 32, 128), BF16),
            pltpu.VMEM((4, 2, 2, 2, 32, 128), BF16),
            pltpu.VMEM((4, 2, 2, 2, 32, 128), BF16),
            pltpu.VMEM((2, 2, 2, 8, 128), F32),
            pltpu.VMEM((2, 2, 4, 4, 64, 128), BF16),
            pltpu.VMEM((2, 2, 2, 64, 128), BF16),
            pltpu.VMEM((2, 2, 2, 64, 128), BF16),
            pltpu.VMEM((2, 2, 4, 64, 128), BF16),
            pltpu.VMEM((2, 2, 4, 64, 128), BF16),
            pltpu.VMEM((2, 2, 4, 64, 128), F32),
            pltpu.VMEM((2, 2, 4, 64, 128), BF16),
            pltpu.VMEM((2, 2, 3, 64, 128), BF16),
            pltpu.VMEM((2, 2, 64, 128), F32),
            pltpu.VMEM((2, 64, 128), BF16),
            pltpu.VMEM((2, 64, 128), BF16),
            pltpu.VMEM((128, 256), F32),
            pltpu.VMEM((128, 128), F32),
            pltpu.VMEM((4, 128, 128), F32),
            pltpu.VMEM((2 * MOST_ROWS, 128), BF16),
            pltpu.SemaphoreType.DMA((N_SENDS,)),
            pltpu.SemaphoreType.DMA((N_RECVS,)),
            pltpu.SemaphoreType.DMA((6,)),
        ],
        compiler_params=pltpu.CompilerParams(
            collective_id=0, has_side_effects=True, vmem_limit_bytes=24 << 20
        ),
        name="cross_layer",
    )(
        *(
            pltpu.with_memory_space_constraint(a, pltpu.HBM)
            for a in (
                base_rows,
                layer_rows.reshape(4, 32, 128),
                upstream,
                cross_bias.reshape(1, 128),
                cross_weight.reshape(4, 2, 4, 2, 128, 128),
            )
        )
    )
    crossed, gbase, glayer, gw, gbias = pl.pallas_call(
        finish,
        out_shape=shapes,
        in_specs=[vmem] * 5,
        out_specs=(pl.BlockSpec(memory_space=pl.ANY),) * 5,
        scratch_shapes=[pltpu.SemaphoreType.DMA((5,))],
        compiler_params=pltpu.CompilerParams(vmem_limit_bytes=4 << 20),
        name="finish",
    )(*results)
    return crossed, gbase, glayer, gw.reshape(1024, 128), gbias.reshape(128)


def solution(mesh):
    return jax.shard_map(
        local,
        mesh=mesh,
        in_specs=(P("dp", "mp"), P("dp", "mp"), P(None, "mp"), P("mp"), P("dp", "mp")),
        out_specs=(P("dp", "mp"), P("dp", "mp"), P("dp", "mp"), P("dp", "mp"), P("mp")),
        check_vma=False,
    )
```

```python
import functools
import math

import jax
import jax.numpy as jnp
from jax import lax
from jax.experimental import pallas as pl
from jax.experimental.pallas import tpu as pltpu
from jax.sharding import PartitionSpec as P

MESH = pl.DeviceIdType.MESH
F32 = jnp.float32
BF16 = jnp.bfloat16
N_SENDS = 14
N_RECVS = 50
MOST_ROWS = 4096


def kernel(
    scale,
    base_hbm,
    lay_hbm,
    up_hbm,
    bias_hbm,
    w4,
    crossed,
    gbase,
    glayer,
    gw,
    gbias,
    base,
    lay,
    up,
    bias,
    wo,
    wp,
    dl,
    dlp,
    xa,
    fs,
    xb,
    do,
    dp_,
    bs,
    part,
    r1lo,
    r1hi,
    rl,
    rr,
    s1,
    b2s,
    r2,
    tt,
    zs,
    zr,
    mixp,
    mixr,
    gws,
    tally,
    send,
    recv,
    lsem,
):
    d = lax.axis_index("dp")
    m = lax.axis_index("mp")
    c = lax.rem(m, 2)
    y = lax.rem(lax.div(m, 2), 4)
    h = lax.rem(lax.div(m, 8), 2)
    x = lax.div(m, 16)
    oh = 1 - h
    oc = 1 - c

    def dev(x_=None, y_=None, h_=None, c_=None, d_=None):
        x_ = x if x_ is None else x_
        y_ = y if y_ is None else y_
        h_ = h if h_ is None else h_
        c_ = c if c_ is None else c_
        d_ = d if d_ is None else d_
        return (d_, ((x_ * 2 + h_) * 4 + y_) * 2 + c_)

    def plus(v, k):
        return lax.rem(v + k, 4)

    ids = iter(range(N_RECVS))
    send_ids = iter(range(N_SENDS))
    sent = [[next(send_ids), 0]]

    def rows(ref):
        return math.prod(ref.shape) * jnp.dtype(ref.dtype).itemsize // 256

    def wait_rows(sem, n):
        view = tally.at[pl.ds(0, n)]
        pltpu.make_async_copy(view, view, sem).wait()

    def put(src, dst, to, k=None):
        k = next(ids) if k is None else k
        n = rows(src)
        if sent[-1][1] + n > MOST_ROWS:
            sent.append([next(send_ids), 0])
        sent[-1][1] += n
        pltpu.make_async_remote_copy(
            src_ref=src,
            dst_ref=dst,
            send_sem=send.at[sent[-1][0]],
            recv_sem=recv.at[k],
            device_id=to,
            device_id_type=MESH,
        ).start()
        return k

    def got(k, *landed):
        wait_rows(recv.at[k], sum(rows(ref) for ref in landed))

    b4, b2, b1 = lax.div(d, 4), lax.rem(lax.div(d, 2), 2), lax.rem(d, 2)

    def first_row(d_, h_):
        window = jnp.clip(d_ - 2, 0, 4)
        return jnp.where(lax.rem(d_, 2) == h_, window, window + 4)

    barrier = pltpu.get_barrier_semaphore()
    near = [dev(c_=oc)]
    near += [dev(x_=plus(x, k)) for k in (1, 2, 3)]
    near += [dev(y_=plus(y, k)) for k in (1, 2, 3)]
    z = h * 8 + d
    for k in range(1, 16):
        zk = lax.rem(z + k, 16)
        near.append(dev(h_=lax.div(zk, 8), d_=lax.rem(zk, 8)))
    for to in near:
        pl.semaphore_signal(barrier, inc=1, device_id=to, device_id_type=MESH)

    loads = [
        pltpu.make_async_copy(src, dst, lsem.at[k])
        for k, (src, dst) in enumerate(
            (
                (lay_hbm, lay),
                (up_hbm, up),
                (base_hbm, base),
                (lay_hbm, xa.at[h, x, y]),
                (bias_hbm, bias),
                (w4.at[:, :, :, c], wo),
            )
        )
    ]
    for load in loads:
        load.start()
    loads[0].wait()
    pl.semaphore_wait(barrier, len(near))

    def ag1(view, n):
        half = n // 2
        a = view(x, y, 0, half)
        b = view(x, y, half, half)
        k = next(ids)
        for j in (1, 3, 2):
            put(a, a, dev(x_=plus(x, j)), k)
            put(b, b, dev(y_=plus(y, j)), k)
        ks = []
        for j in (1, 3):
            ks.append((put(a, a, dev(y_=plus(y, j))), put(b, b, dev(x_=plus(x, j)))))
        return k, ks

    every = pl.ds(0, 4)

    def ag2(view, n, sent1):
        half = n // 2
        k, ks = sent1
        got(k, *[view(x, y, 0, half)] * 3, *[view(x, y, half, half)] * 3)
        for (ka, kb), j in zip(ks, (1, 3), strict=True):
            for i in (1, 3, 2):
                a = view(plus(x, i), y, 0, half)
                b = view(x, plus(y, i), half, half)
                put(a, a, dev(y_=plus(y, j)), ka)
                put(b, b, dev(x_=plus(x, j)), kb)
        return ks

    def ag2_forward(view, n, ks):
        half = n // 2
        k = next(ids)
        for (ka, kb), j, part_of in zip(ks, (1, 3), (pl.ds(0, 2), pl.ds(2, 2)), strict=True):
            ys, xs = plus(y, 4 - j), plus(x, 4 - j)
            got(ka, view(every, ys, 0, half))
            a = view(part_of, ys, 0, half)
            put(a, a, dev(y_=plus(y, j)), k)
            got(kb, view(xs, every, half, half))
            b = view(xs, part_of, half, half)
            put(b, b, dev(x_=plus(x, j)), k)
        return k

    def ag2_wait(view, n, k):
        half = n // 2
        got(k, view(every, y, 0, half), view(x, every, half, half))

    def x_own(xs, ys, q, nq):
        return xa.at[h, xs, ys, pl.ds(q, nq)]

    def x_other(xs, ys, q, nq):
        return xa.at[oh, xs, ys, pl.ds(q, nq)]

    def x_block0(xs, ys, q, nq):
        return xb.at[xs, ys, pl.ds(q, nq)]

    def x_block1(xs, ys, q, nq):
        return xb.at[xs, ys, pl.ds(4 + q, nq)]

    k_zx = put(lay, xa.at[h, x, y], dev(h_=oh))
    k_fs = next(ids)
    for j in (2, 1, 3):
        t = plus(x, j)
        put(lay.at[t], fs.at[x], dev(x_=t), k_fs)
    z_first = [next(send_ids) for _ in range(8)]
    z_recv = next(ids)
    next(ids)
    z_sent = []

    def along_z_to_block(j):
        s = plus(x, j)
        src = lay.at[x] if j == 0 else fs.at[s]
        d_to = 2 * s + h
        for hh in (0, 1):
            n = 2 * j + hh
            same = jnp.logical_and(h == hh, d_to == d)
            slot = lax.rem(d + 8 - first_row(d_to, hh), 8)
            dst = xb.at[x, y, slot]
            copy = pltpu.make_async_remote_copy(
                src_ref=src,
                dst_ref=dst,
                send_sem=send.at[z_first[n]],
                recv_sem=recv.at[z_recv + lax.div(slot, 4)],
                device_id=dev(h_=hh, d_=d_to),
                device_id_type=MESH,
            )
            stay = pltpu.make_async_copy(src, dst, recv.at[z_recv + lax.div(slot, 4)])

            @pl.when(same)
            def _(stay=stay):
                stay.start()

            @pl.when(jnp.logical_not(same))
            def _(copy=copy):
                copy.start()

            z_sent.append((same, copy))

    along_z_to_block(0)

    k_wp = [put(w4.at[:, oh, :, oc], wp.at[:, oh], dev(c_=oc))]
    loads[3].wait()
    own1 = ag1(x_own, 4)

    loads[1].wait()
    loads[2].wait()
    upper = up[...].astype(F32)
    basef = base[...].astype(F32)
    delta = upper * basef
    low = delta.astype(BF16).reshape(4, 32, 128)
    dl[...] = low
    do[:, b4, b2, b1] = low
    bs[b4, b2, b1] = jnp.broadcast_to(jnp.sum(delta, axis=0, keepdims=True), (8, 128))
    k_dlp = put(dl, dlp, dev(c_=oc))

    every2 = pl.ds(0, 2)
    steps = (
        (dev(d_=d + 4 - 8 * b4), (b4, b2, b1), (1 - b4, b2, b1)),
        (dev(d_=d + 2 - 4 * b2), (every2, b2, b1), (every2, 1 - b2, b1)),
        (dev(d_=d + 1 - 2 * b1), (every2, every2, b1), (every2, every2, 1 - b1)),
    )

    def along_z(step):
        to, here, _ = steps[step]
        a, b = do.at[(slice(None), *here)], bs.at[here]
        return put(b, b, to, put(a, a, to))

    def along_z_wait(step, k):
        theirs = steps[step][2]
        got(k, do.at[(slice(None), *theirs)], bs.at[theirs])

    k_d = along_z(0)
    k_wp.append(put(w4.at[:, h, :, oc], wp.at[:, h], dev(c_=oc)))

    loads[5].wait()
    got(k_dlp, dlp)
    d_own = dl[...].reshape(128, 128)
    d_other = dlp[...].reshape(128, 128)
    nt = (((1,), (1,)), ((), ()))
    lo, hi = pl.ds(0, 2), pl.ds(2, 2)

    def to_line(half, j):
        return dev(x_=plus(x, j)) if half == 0 else dev(y_=plus(y, j))

    def to_line2(half, j):
        return dev(y_=plus(y, j)) if half == 0 else dev(x_=plus(x, j))

    def back_terms(hs):
        for xs in range(4):
            term = lax.dot_general(
                wo[xs, hs].reshape(512, 128), d_own, nt, preferred_element_type=F32
            ) + lax.dot_general(
                wp[xs, hs].reshape(512, 128), d_other, nt, preferred_element_type=F32
            )
            term = term.astype(BF16).reshape(4, 128, 128)
            part[hs, 0, xs] = term[:, 0:64]
            for ys in range(4):
                part[hs, 1, ys, xs] = term[ys, 64:128]

    def rs1(hs):
        first, rest = [], next(ids)
        for half in (0, 1):
            me = x if half == 0 else y
            a = put(part.at[hs, half, plus(me, 2), lo], r1lo.at[hs, half], to_line(half, 1))
            b = put(part.at[hs, half, plus(me, 2), hi], r1hi.at[hs, half], to_line(half, 3))
            first.append((a, b))
        for half in (0, 1):
            me = x if half == 0 else y
            put(part.at[hs, half, plus(me, 1), hi], rl.at[hs, half, hi], to_line(half, 1), rest)
            put(part.at[hs, half, plus(me, 3), lo], rr.at[hs, half, lo], to_line(half, 3), rest)
        return first, rest

    def rs2(hs, ks):
        first, rest = ks
        for half in (0, 1):
            me = x if half == 0 else y
            a, b = first[half]
            got(a, r1lo.at[hs, half])
            t = plus(me, 1)
            part[hs, half, t, lo] = (
                part[hs, half, t, lo].astype(F32) + r1lo[hs, half].astype(F32)
            ).astype(BF16)
            put(part.at[hs, half, t, lo], rl.at[hs, half, lo], to_line(half, 1), rest)
            got(b, r1hi.at[hs, half])
            t = plus(me, 3)
            part[hs, half, t, hi] = (
                part[hs, half, t, hi].astype(F32) + r1hi[hs, half].astype(F32)
            ).astype(BF16)
            put(part.at[hs, half, t, hi], rr.at[hs, half, hi], to_line(half, 3), rest)
        return rest

    def rs3(hs, rest):
        got(rest, rl.at[hs], rr.at[hs])
        k = next(ids)
        for half in (0, 1):
            me, me2 = (x, y) if half == 0 else (y, x)
            total = (
                part[hs, half, me].astype(F32)
                + rl[hs, half].astype(F32)
                + rr[hs, half].astype(F32)
            )
            s1[hs, half] = total
            b2s[hs, half] = total.astype(BF16)
            for j in (1, 3, 2):
                t = plus(me2, j)
                put(b2s.at[hs, half, t], r2.at[hs, half, j - 1], to_line2(half, j), k)
        return k

    def rs4(hs, k):
        got(k, r2.at[hs])
        for half in (0, 1):
            me2 = y if half == 0 else x
            tt[hs, half] = (
                s1[hs, half, me2]
                + r2[hs, half, 0].astype(F32)
                + r2[hs, half, 1].astype(F32)
                + r2[hs, half, 2].astype(F32)
            )

    got(k_wp[0], wp.at[:, oh])
    back_terms(oh)
    k_far = rs1(oh)
    got(k_wp[1], wp.at[:, h])
    back_terms(h)
    k_near = rs1(h)

    got(k_fs, lay.at[pl.ds(0, 3)])
    for j in (1, 2, 3):
        along_z_to_block(j)
    k_far = rs2(oh, k_far)
    k_near = rs2(h, k_near)
    own2 = ag2(x_own, 4, own1)

    def mixed_terms(hs, acc):
        for xs in range(4):
            rows = jnp.concatenate([xa[hs, xs, ys].reshape(128, 128) for ys in range(4)], axis=1)
            cols = jnp.concatenate(
                [wo[xs, hs].reshape(512, 128), wp[xs, hs].reshape(512, 128)], axis=1
            )
            acc = acc + jnp.dot(rows, cols, preferred_element_type=F32)
        return acc

    quarter = xb.at[x, y, pl.ds(0, 4)]
    got(k_zx, xa.at[oh, x, y])
    other1 = ag1(x_other, 4)
    got(z_recv, quarter)
    first1 = ag1(x_block0, 4)
    k_far = rs3(oh, k_far)
    along_z_wait(0, k_d)
    k_d = along_z(1)
    got(z_recv + 1, quarter)
    second1 = ag1(x_block1, 4)
    k_near = rs3(h, k_near)

    own3 = ag2_forward(x_own, 4, own2)
    first2 = ag2(x_block0, 4, first1)
    other2 = ag2(x_other, 4, other1)
    along_z_wait(1, k_d)
    k_d = along_z(2)

    rs4(oh, k_far)
    zs[...] = tt[oh].astype(BF16)
    k_zr = put(zs, zr, dev(h_=oh))

    second2 = ag2(x_block1, 4, second1)
    ag2_wait(x_own, 4, own3)
    mixp[...] = mixed_terms(h, jnp.zeros((128, 256), F32))

    first3 = ag2_forward(x_block0, 4, first2)
    other3 = ag2_forward(x_other, 4, other2)
    rs4(h, k_near)
    second3 = ag2_forward(x_block1, 4, second2)
    along_z_wait(2, k_d)
    k_dp = put(do, dp_, dev(c_=oc))

    ag2_wait(x_other, 4, other3)
    mixp[...] = mixed_terms(oh, mixp[...])
    k_mix = put(mixp.at[:, pl.ds(128, 128)], mixr, dev(c_=oc))

    tn = (((0,), (0,)), ((), ()))

    def rows_of(ref, xs, g):
        out = []
        for k in range(4):
            s = lax.rem(first_row(d, h) + 4 * g + k, 8)
            out.append(ref[xs, lax.div(s, 4), lax.rem(lax.div(s, 2), 2), lax.rem(s, 2)])
        return jnp.concatenate(out, axis=0)

    def weight_terms(g, ref):
        feats = jnp.concatenate(
            [
                jnp.concatenate(
                    [xb[xs, ys, 4 * g : 4 * g + 4].reshape(128, 128) for ys in range(4)], axis=1
                )
                for xs in range(4)
            ],
            axis=0,
        )
        cols = jnp.concatenate([rows_of(ref, xs, g) for xs in range(4)], axis=0)
        return lax.dot_general(feats, cols, tn, preferred_element_type=F32)

    got(k_dp, dp_)
    ag2_wait(x_block0, 4, first3)
    theirs, ours = weight_terms(0, dp_), weight_terms(0, do)
    ag2_wait(x_block1, 4, second3)
    theirs = theirs + weight_terms(1, dp_)
    gws[...] = (theirs * scale).reshape(4, 128, 128)
    k_gw = put(gws, gw.at[:, c], dev(c_=oc))
    ours = ours + weight_terms(1, do)
    gw[:, c] = (ours * scale).reshape(4, 128, 128)

    gbias[...] = jnp.sum(bs[...].reshape(8, 8, 128)[:, 0], axis=0, keepdims=True) * scale

    got(k_mix, mixr)
    loads[4].wait()
    mixed = mixp[:, 0:128] + mixr[...] + bias[...]
    crossed[...] = (basef * mixed + lay[...].reshape(128, 128).astype(F32)).astype(BF16)
    gbase[...] = (upper * mixed).astype(BF16)

    got(k_zr, zr)
    back = (tt[h] + zr[...].astype(F32)).reshape(128, 128)
    glayer[...] = (upper + back.T).astype(BF16)

    got(k_gw, gw.at[:, oc])
    for k, n in sent:
        wait_rows(send.at[k], n)
    for same, copy in z_sent:

        @pl.when(jnp.logical_not(same))
        def _(copy=copy):
            copy.wait_send()


def finish(a, b, e, g, s, oa, ob, oe, og, os_, sem):
    copies = [
        pltpu.make_async_copy(src, dst, sem.at[k])
        for k, (src, dst) in enumerate(((g, og), (a, oa), (b, ob), (e, oe), (s, os_)))
    ]
    for copy in copies:
        copy.start()
    for copy in copies:
        copy.wait()


def local(base_rows, layer_rows, cross_weight, cross_bias, upstream):
    vmem = pl.BlockSpec(memory_space=pltpu.VMEM)
    hbm = pl.BlockSpec(memory_space=pltpu.HBM)
    scale = float((base_rows.shape[0] * 8) ** -0.5)
    small = jax.ShapeDtypeStruct((128, 128), BF16)
    shapes = (
        small,
        small,
        small,
        jax.ShapeDtypeStruct((4, 2, 128, 128), F32),
        jax.ShapeDtypeStruct((1, 128), F32),
    )
    results = pl.pallas_call(
        functools.partial(kernel, scale),
        out_shape=shapes,
        in_specs=[hbm] * 5,
        out_specs=(vmem, vmem, vmem, vmem, vmem),
        scratch_shapes=[
            pltpu.VMEM((128, 128), BF16),
            pltpu.VMEM((4, 32, 128), BF16),
            pltpu.VMEM((128, 128), BF16),
            pltpu.VMEM((1, 128), F32),
            pltpu.VMEM((4, 2, 4, 128, 128), BF16),
            pltpu.VMEM((4, 2, 4, 128, 128), BF16),
            pltpu.VMEM((4, 32, 128), BF16),
            pltpu.VMEM((4, 32, 128), BF16),
            pltpu.VMEM((2, 4, 4, 4, 32, 128), BF16),
            pltpu.VMEM((4, 32, 128), BF16),
            pltpu.VMEM((4, 4, 8, 32, 128), BF16),
            pltpu.VMEM((4, 2, 2, 2, 32, 128), BF16),
            pltpu.VMEM((4, 2, 2, 2, 32, 128), BF16),
            pltpu.VMEM((2, 2, 2, 8, 128), F32),
            pltpu.VMEM((2, 2, 4, 4, 64, 128), BF16),
            pltpu.VMEM((2, 2, 2, 64, 128), BF16),
            pltpu.VMEM((2, 2, 2, 64, 128), BF16),
            pltpu.VMEM((2, 2, 4, 64, 128), BF16),
            pltpu.VMEM((2, 2, 4, 64, 128), BF16),
            pltpu.VMEM((2, 2, 4, 64, 128), F32),
            pltpu.VMEM((2, 2, 4, 64, 128), BF16),
            pltpu.VMEM((2, 2, 3, 64, 128), BF16),
            pltpu.VMEM((2, 2, 64, 128), F32),
            pltpu.VMEM((2, 64, 128), BF16),
            pltpu.VMEM((2, 64, 128), BF16),
            pltpu.VMEM((128, 256), F32),
            pltpu.VMEM((128, 128), F32),
            pltpu.VMEM((4, 128, 128), F32),
            pltpu.VMEM((2 * MOST_ROWS, 128), BF16),
            pltpu.SemaphoreType.DMA((N_SENDS,)),
            pltpu.SemaphoreType.DMA((N_RECVS,)),
            pltpu.SemaphoreType.DMA((6,)),
        ],
        compiler_params=pltpu.CompilerParams(
            collective_id=0, has_side_effects=True, vmem_limit_bytes=24 << 20
        ),
        name="cross_layer",
    )(
        *(
            pltpu.with_memory_space_constraint(a, pltpu.HBM)
            for a in (
                base_rows,
                layer_rows.reshape(4, 32, 128),
                upstream,
                cross_bias.reshape(1, 128),
                cross_weight.reshape(4, 2, 4, 2, 128, 128),
            )
        )
    )
    crossed, gbase, glayer, gw, gbias = pl.pallas_call(
        finish,
        out_shape=shapes,
        in_specs=[vmem] * 5,
        out_specs=(pl.BlockSpec(memory_space=pl.ANY),) * 5,
        scratch_shapes=[pltpu.SemaphoreType.DMA((5,))],
        compiler_params=pltpu.CompilerParams(vmem_limit_bytes=4 << 20),
        name="finish",
    )(*results)
    return crossed, gbase, glayer, gw.reshape(1024, 128), gbias.reshape(128)


def solution(mesh):
    return jax.shard_map(
        local,
        mesh=mesh,
        in_specs=(P("dp", "mp"), P("dp", "mp"), P(None, "mp"), P("mp"), P("dp", "mp")),
        out_specs=(P("dp", "mp"), P("dp", "mp"), P("dp", "mp"), P("dp", "mp"), P("mp")),
        check_vma=False,
    )
```

```python
import functools
import math

import jax
import jax.numpy as jnp
from jax import lax
from jax.experimental import pallas as pl
from jax.experimental.pallas import tpu as pltpu
from jax.sharding import PartitionSpec as P

MESH = pl.DeviceIdType.MESH
F32 = jnp.float32
BF16 = jnp.bfloat16
N_SENDS = 14
N_RECVS = 50
MOST_ROWS = 4096


def kernel(
    scale,
    base_hbm,
    lay_hbm,
    up_hbm,
    bias_hbm,
    w4,
    crossed,
    gbase,
    glayer,
    gw,
    gbias,
    base,
    lay,
    up,
    bias,
    wo,
    wp,
    dl,
    dlp,
    xa,
    fs,
    xb,
    do,
    dp_,
    bs,
    part,
    r1lo,
    r1hi,
    rl,
    rr,
    s1,
    b2s,
    r2,
    tt,
    zs,
    zr,
    mixp,
    mixr,
    gws,
    tally,
    send,
    recv,
    lsem,
):
    d = lax.axis_index("dp")
    m = lax.axis_index("mp")
    c = lax.rem(m, 2)
    y = lax.rem(lax.div(m, 2), 4)
    h = lax.rem(lax.div(m, 8), 2)
    x = lax.div(m, 16)
    oh = 1 - h
    oc = 1 - c

    def dev(x_=None, y_=None, h_=None, c_=None, d_=None):
        x_ = x if x_ is None else x_
        y_ = y if y_ is None else y_
        h_ = h if h_ is None else h_
        c_ = c if c_ is None else c_
        d_ = d if d_ is None else d_
        return (d_, ((x_ * 2 + h_) * 4 + y_) * 2 + c_)

    def plus(v, k):
        return lax.rem(v + k, 4)

    ids = iter(range(N_RECVS))
    send_ids = iter(range(N_SENDS))
    sent = [[next(send_ids), 0]]

    def rows(ref):
        return math.prod(ref.shape) * jnp.dtype(ref.dtype).itemsize // 256

    def wait_rows(sem, n):
        view = tally.at[pl.ds(0, n)]
        pltpu.make_async_copy(view, view, sem).wait()

    def put(src, dst, to, k=None):
        k = next(ids) if k is None else k
        n = rows(src)
        if sent[-1][1] + n > MOST_ROWS:
            sent.append([next(send_ids), 0])
        sent[-1][1] += n
        pltpu.make_async_remote_copy(
            src_ref=src,
            dst_ref=dst,
            send_sem=send.at[sent[-1][0]],
            recv_sem=recv.at[k],
            device_id=to,
            device_id_type=MESH,
        ).start()
        return k

    def got(k, *landed):
        wait_rows(recv.at[k], sum(rows(ref) for ref in landed))

    b4, b2, b1 = lax.div(d, 4), lax.rem(lax.div(d, 2), 2), lax.rem(d, 2)

    def first_row(d_, h_):
        window = jnp.clip(d_ - 2, 0, 4)
        return jnp.where(lax.rem(d_, 2) == h_, window, window + 4)

    barrier = pltpu.get_barrier_semaphore()
    near = []
    z = h * 8 + d
    for k in (8, 7, 9, 6, 10, 5, 11, 4, 12, 3, 13, 2, 14, 1, 15):
        zk = lax.rem(z + k, 16)
        near.append(dev(h_=lax.div(zk, 8), d_=lax.rem(zk, 8)))
    near += [dev(x_=plus(x, k)) for k in (2, 1, 3)]
    near += [dev(y_=plus(y, k)) for k in (2, 1, 3)]
    near.append(dev(c_=oc))
    for to in near:
        pl.semaphore_signal(barrier, inc=1, device_id=to, device_id_type=MESH)

    loads = [
        pltpu.make_async_copy(src, dst, lsem.at[k])
        for k, (src, dst) in enumerate(
            (
                (lay_hbm, lay),
                (up_hbm, up),
                (base_hbm, base),
                (lay_hbm, xa.at[h, x, y]),
                (bias_hbm, bias),
                (w4.at[:, :, :, c], wo),
            )
        )
    ]
    for load in loads:
        load.start()
    loads[0].wait()
    pl.semaphore_wait(barrier, len(near))

    def ag1(view, n):
        half = n // 2
        a = view(x, y, 0, half)
        b = view(x, y, half, half)
        k = next(ids)
        for j in (1, 3, 2):
            put(a, a, dev(x_=plus(x, j)), k)
            put(b, b, dev(y_=plus(y, j)), k)
        ks = []
        for j in (1, 3):
            ks.append((put(a, a, dev(y_=plus(y, j))), put(b, b, dev(x_=plus(x, j)))))
        return k, ks

    every = pl.ds(0, 4)

    def ag2(view, n, sent1):
        half = n // 2
        k, ks = sent1
        got(k, *[view(x, y, 0, half)] * 3, *[view(x, y, half, half)] * 3)
        for (ka, kb), j in zip(ks, (1, 3), strict=True):
            for i in (1, 3, 2):
                a = view(plus(x, i), y, 0, half)
                b = view(x, plus(y, i), half, half)
                put(a, a, dev(y_=plus(y, j)), ka)
                put(b, b, dev(x_=plus(x, j)), kb)
        return ks

    def ag2_forward(view, n, ks):
        half = n // 2
        k = next(ids)
        for (ka, kb), j, part_of in zip(ks, (1, 3), (pl.ds(0, 2), pl.ds(2, 2)), strict=True):
            ys, xs = plus(y, 4 - j), plus(x, 4 - j)
            got(ka, view(every, ys, 0, half))
            a = view(part_of, ys, 0, half)
            put(a, a, dev(y_=plus(y, j)), k)
            got(kb, view(xs, every, half, half))
            b = view(xs, part_of, half, half)
            put(b, b, dev(x_=plus(x, j)), k)
        return k

    def ag2_wait(view, n, k):
        half = n // 2
        got(k, view(every, y, 0, half), view(x, every, half, half))

    def x_own(xs, ys, q, nq):
        return xa.at[h, xs, ys, pl.ds(q, nq)]

    def x_other(xs, ys, q, nq):
        return xa.at[oh, xs, ys, pl.ds(q, nq)]

    def x_block0(xs, ys, q, nq):
        return xb.at[xs, ys, pl.ds(q, nq)]

    def x_block1(xs, ys, q, nq):
        return xb.at[xs, ys, pl.ds(4 + q, nq)]

    k_zx = put(lay, xa.at[h, x, y], dev(h_=oh))
    k_fs = next(ids)
    for j in (2, 1, 3):
        t = plus(x, j)
        put(lay.at[t], fs.at[x], dev(x_=t), k_fs)
    z_first = [next(send_ids) for _ in range(8)]
    z_recv = next(ids)
    next(ids)
    z_sent = []

    def along_z_to_block(j):
        s = plus(x, j)
        src = lay.at[x] if j == 0 else fs.at[s]
        d_to = 2 * s + h
        for hh in (0, 1):
            n = 2 * j + hh
            same = jnp.logical_and(h == hh, d_to == d)
            slot = lax.rem(d + 8 - first_row(d_to, hh), 8)
            dst = xb.at[x, y, slot]
            copy = pltpu.make_async_remote_copy(
                src_ref=src,
                dst_ref=dst,
                send_sem=send.at[z_first[n]],
                recv_sem=recv.at[z_recv + lax.div(slot, 4)],
                device_id=dev(h_=hh, d_=d_to),
                device_id_type=MESH,
            )
            stay = pltpu.make_async_copy(src, dst, recv.at[z_recv + lax.div(slot, 4)])

            @pl.when(same)
            def _(stay=stay):
                stay.start()

            @pl.when(jnp.logical_not(same))
            def _(copy=copy):
                copy.start()

            z_sent.append((same, copy))

    along_z_to_block(0)

    k_wp = [put(w4.at[:, oh, :, oc], wp.at[:, oh], dev(c_=oc))]
    loads[3].wait()
    own1 = ag1(x_own, 4)

    loads[1].wait()
    loads[2].wait()
    upper = up[...].astype(F32)
    basef = base[...].astype(F32)
    delta = upper * basef
    low = delta.astype(BF16).reshape(4, 32, 128)
    dl[...] = low
    do[:, b4, b2, b1] = low
    bs[b4, b2, b1] = jnp.broadcast_to(jnp.sum(delta, axis=0, keepdims=True), (8, 128))
    k_dlp = put(dl, dlp, dev(c_=oc))

    every2 = pl.ds(0, 2)
    steps = (
        (dev(d_=d + 4 - 8 * b4), (b4, b2, b1), (1 - b4, b2, b1)),
        (dev(d_=d + 2 - 4 * b2), (every2, b2, b1), (every2, 1 - b2, b1)),
        (dev(d_=d + 1 - 2 * b1), (every2, every2, b1), (every2, every2, 1 - b1)),
    )

    def along_z(step):
        to, here, _ = steps[step]
        a, b = do.at[(slice(None), *here)], bs.at[here]
        return put(b, b, to, put(a, a, to))

    def along_z_wait(step, k):
        theirs = steps[step][2]
        got(k, do.at[(slice(None), *theirs)], bs.at[theirs])

    k_d = along_z(0)
    k_wp.append(put(w4.at[:, h, :, oc], wp.at[:, h], dev(c_=oc)))

    loads[5].wait()
    got(k_dlp, dlp)
    d_own = dl[...].reshape(128, 128)
    d_other = dlp[...].reshape(128, 128)
    nt = (((1,), (1,)), ((), ()))
    lo, hi = pl.ds(0, 2), pl.ds(2, 2)

    def to_line(half, j):
        return dev(x_=plus(x, j)) if half == 0 else dev(y_=plus(y, j))

    def to_line2(half, j):
        return dev(y_=plus(y, j)) if half == 0 else dev(x_=plus(x, j))

    def back_terms(hs):
        for xs in range(4):
            term = lax.dot_general(
                wo[xs, hs].reshape(512, 128), d_own, nt, preferred_element_type=F32
            ) + lax.dot_general(
                wp[xs, hs].reshape(512, 128), d_other, nt, preferred_element_type=F32
            )
            term = term.astype(BF16).reshape(4, 128, 128)
            part[hs, 0, xs] = term[:, 0:64]
            for ys in range(4):
                part[hs, 1, ys, xs] = term[ys, 64:128]

    def rs1(hs):
        first, rest = [], next(ids)
        for half in (0, 1):
            me = x if half == 0 else y
            a = put(part.at[hs, half, plus(me, 2), lo], r1lo.at[hs, half], to_line(half, 1))
            b = put(part.at[hs, half, plus(me, 2), hi], r1hi.at[hs, half], to_line(half, 3))
            first.append((a, b))
        for half in (0, 1):
            me = x if half == 0 else y
            put(part.at[hs, half, plus(me, 1), hi], rl.at[hs, half, hi], to_line(half, 1), rest)
            put(part.at[hs, half, plus(me, 3), lo], rr.at[hs, half, lo], to_line(half, 3), rest)
        return first, rest

    def rs2(hs, ks):
        first, rest = ks
        for half in (0, 1):
            me = x if half == 0 else y
            a, b = first[half]
            got(a, r1lo.at[hs, half])
            t = plus(me, 1)
            part[hs, half, t, lo] = (
                part[hs, half, t, lo].astype(F32) + r1lo[hs, half].astype(F32)
            ).astype(BF16)
            put(part.at[hs, half, t, lo], rl.at[hs, half, lo], to_line(half, 1), rest)
            got(b, r1hi.at[hs, half])
            t = plus(me, 3)
            part[hs, half, t, hi] = (
                part[hs, half, t, hi].astype(F32) + r1hi[hs, half].astype(F32)
            ).astype(BF16)
            put(part.at[hs, half, t, hi], rr.at[hs, half, hi], to_line(half, 3), rest)
        return rest

    def rs3(hs, rest):
        got(rest, rl.at[hs], rr.at[hs])
        k = next(ids)
        for half in (0, 1):
            me, me2 = (x, y) if half == 0 else (y, x)
            total = (
                part[hs, half, me].astype(F32)
                + rl[hs, half].astype(F32)
                + rr[hs, half].astype(F32)
            )
            s1[hs, half] = total
            b2s[hs, half] = total.astype(BF16)
            for j in (1, 3, 2):
                t = plus(me2, j)
                put(b2s.at[hs, half, t], r2.at[hs, half, j - 1], to_line2(half, j), k)
        return k

    def rs4(hs, k):
        got(k, r2.at[hs])
        for half in (0, 1):
            me2 = y if half == 0 else x
            tt[hs, half] = (
                s1[hs, half, me2]
                + r2[hs, half, 0].astype(F32)
                + r2[hs, half, 1].astype(F32)
                + r2[hs, half, 2].astype(F32)
            )

    got(k_wp[0], wp.at[:, oh])
    back_terms(oh)
    k_far = rs1(oh)
    got(k_wp[1], wp.at[:, h])
    back_terms(h)
    k_near = rs1(h)

    got(k_fs, lay.at[pl.ds(0, 3)])
    for j in (1, 2, 3):
        along_z_to_block(j)
    own2 = ag2(x_own, 4, own1)
    k_far = rs2(oh, k_far)
    k_near = rs2(h, k_near)

    def mixed_terms(hs, acc):
        for xs in range(4):
            rows = jnp.concatenate([xa[hs, xs, ys].reshape(128, 128) for ys in range(4)], axis=1)
            cols = jnp.concatenate(
                [wo[xs, hs].reshape(512, 128), wp[xs, hs].reshape(512, 128)], axis=1
            )
            acc = acc + jnp.dot(rows, cols, preferred_element_type=F32)
        return acc

    quarter = xb.at[x, y, pl.ds(0, 4)]
    got(k_zx, xa.at[oh, x, y])
    other1 = ag1(x_other, 4)
    got(z_recv, quarter)
    first1 = ag1(x_block0, 4)
    own3 = ag2_forward(x_own, 4, own2)
    k_far = rs3(oh, k_far)
    along_z_wait(0, k_d)
    k_d = along_z(1)
    got(z_recv + 1, quarter)
    second1 = ag1(x_block1, 4)
    k_near = rs3(h, k_near)

    first2 = ag2(x_block0, 4, first1)
    other2 = ag2(x_other, 4, other1)
    along_z_wait(1, k_d)
    k_d = along_z(2)

    rs4(oh, k_far)
    zs[...] = tt[oh].astype(BF16)
    k_zr = put(zs, zr, dev(h_=oh))

    second2 = ag2(x_block1, 4, second1)
    ag2_wait(x_own, 4, own3)
    mixp[...] = mixed_terms(h, jnp.zeros((128, 256), F32))

    first3 = ag2_forward(x_block0, 4, first2)
    other3 = ag2_forward(x_other, 4, other2)
    rs4(h, k_near)
    second3 = ag2_forward(x_block1, 4, second2)
    along_z_wait(2, k_d)
    k_dp = put(do, dp_, dev(c_=oc))

    ag2_wait(x_other, 4, other3)
    mixp[...] = mixed_terms(oh, mixp[...])
    k_mix = put(mixp.at[:, pl.ds(128, 128)], mixr, dev(c_=oc))


    def rows_of(ref, xs, g):
        out = []
        for k in range(4):
            s = lax.rem(first_row(d, h) + 4 * g + k, 8)
            out.append(ref[xs, lax.div(s, 4), lax.rem(lax.div(s, 2), 2), lax.rem(s, 2)])
        return jnp.concatenate(out, axis=0)

    def features(g):
        return jnp.concatenate(
            [
                jnp.concatenate(
                    [xb[xs, ys, 4 * g : 4 * g + 4].reshape(128, 128) for ys in range(4)], axis=1
                ).T
                for xs in range(4)
            ],
            axis=1,
        )

    def weight_terms(feats, g, ref):
        cols = jnp.concatenate([rows_of(ref, xs, g) for xs in range(4)], axis=0)
        return jnp.dot(feats, cols, preferred_element_type=F32)

    got(k_dp, dp_)
    ag2_wait(x_block0, 4, first3)
    feats = features(0)
    gws[...] = weight_terms(feats, 0, dp_).reshape(4, 128, 128)
    gw[:, c] = weight_terms(feats, 0, do).reshape(4, 128, 128)
    ag2_wait(x_block1, 4, second3)
    feats = features(1)
    gws[...] = (gws[...] + weight_terms(feats, 1, dp_).reshape(4, 128, 128)) * scale
    k_gw = put(gws, gw.at[:, c], dev(c_=oc))
    gw[:, c] = (gw[:, c] + weight_terms(feats, 1, do).reshape(4, 128, 128)) * scale

    gbias[...] = jnp.sum(bs[...].reshape(8, 8, 128)[:, 0], axis=0, keepdims=True) * scale

    got(k_mix, mixr)
    loads[4].wait()
    mixed = mixp[:, 0:128] + mixr[...] + bias[...]
    crossed[...] = (basef * mixed + lay[...].reshape(128, 128).astype(F32)).astype(BF16)
    gbase[...] = (upper * mixed).astype(BF16)

    got(k_zr, zr)
    back = (tt[h] + zr[...].astype(F32)).reshape(128, 128)
    glayer[...] = (upper + back.T).astype(BF16)

    got(k_gw, gw.at[:, oc])
    for k, n in sent:
        wait_rows(send.at[k], n)
    for same, copy in z_sent:

        @pl.when(jnp.logical_not(same))
        def _(copy=copy):
            copy.wait_send()


def finish(a, b, e, g, s, oa, ob, oe, og, os_, sem):
    copies = [
        pltpu.make_async_copy(src, dst, sem.at[k])
        for k, (src, dst) in enumerate(
            (
                (g.at[0], og.at[0]),
                (g.at[1], og.at[1]),
                (g.at[2], og.at[2]),
                (g.at[3], og.at[3]),
                (a, oa),
                (b, ob),
                (e, oe),
                (s, os_),
            )
        )
    ]
    for copy in copies:
        copy.start()
    for copy in copies:
        copy.wait()


def local(base_rows, layer_rows, cross_weight, cross_bias, upstream):
    vmem = pl.BlockSpec(memory_space=pltpu.VMEM)
    hbm = pl.BlockSpec(memory_space=pltpu.HBM)
    scale = float((base_rows.shape[0] * 8) ** -0.5)
    small = jax.ShapeDtypeStruct((128, 128), BF16)
    shapes = (
        small,
        small,
        small,
        jax.ShapeDtypeStruct((4, 2, 128, 128), F32),
        jax.ShapeDtypeStruct((1, 128), F32),
    )
    results = pl.pallas_call(
        functools.partial(kernel, scale),
        out_shape=shapes,
        in_specs=[hbm] * 5,
        out_specs=(vmem, vmem, vmem, vmem, vmem),
        scratch_shapes=[
            pltpu.VMEM((128, 128), BF16),
            pltpu.VMEM((4, 32, 128), BF16),
            pltpu.VMEM((128, 128), BF16),
            pltpu.VMEM((1, 128), F32),
            pltpu.VMEM((4, 2, 4, 128, 128), BF16),
            pltpu.VMEM((4, 2, 4, 128, 128), BF16),
            pltpu.VMEM((4, 32, 128), BF16),
            pltpu.VMEM((4, 32, 128), BF16),
            pltpu.VMEM((2, 4, 4, 4, 32, 128), BF16),
            pltpu.VMEM((4, 32, 128), BF16),
            pltpu.VMEM((4, 4, 8, 32, 128), BF16),
            pltpu.VMEM((4, 2, 2, 2, 32, 128), BF16),
            pltpu.VMEM((4, 2, 2, 2, 32, 128), BF16),
            pltpu.VMEM((2, 2, 2, 8, 128), F32),
            pltpu.VMEM((2, 2, 4, 4, 64, 128), BF16),
            pltpu.VMEM((2, 2, 2, 64, 128), BF16),
            pltpu.VMEM((2, 2, 2, 64, 128), BF16),
            pltpu.VMEM((2, 2, 4, 64, 128), BF16),
            pltpu.VMEM((2, 2, 4, 64, 128), BF16),
            pltpu.VMEM((2, 2, 4, 64, 128), F32),
            pltpu.VMEM((2, 2, 4, 64, 128), BF16),
            pltpu.VMEM((2, 2, 3, 64, 128), BF16),
            pltpu.VMEM((2, 2, 64, 128), F32),
            pltpu.VMEM((2, 64, 128), BF16),
            pltpu.VMEM((2, 64, 128), BF16),
            pltpu.VMEM((128, 256), F32),
            pltpu.VMEM((128, 128), F32),
            pltpu.VMEM((4, 128, 128), F32),
            pltpu.VMEM((2 * MOST_ROWS, 128), BF16),
            pltpu.SemaphoreType.DMA((N_SENDS,)),
            pltpu.SemaphoreType.DMA((N_RECVS,)),
            pltpu.SemaphoreType.DMA((6,)),
        ],
        compiler_params=pltpu.CompilerParams(
            collective_id=0, has_side_effects=True, vmem_limit_bytes=24 << 20
        ),
        name="cross_layer",
    )(
        *(
            pltpu.with_memory_space_constraint(a, pltpu.HBM)
            for a in (
                base_rows,
                layer_rows.reshape(4, 32, 128),
                upstream,
                cross_bias.reshape(1, 128),
                cross_weight.reshape(4, 2, 4, 2, 128, 128),
            )
        )
    )
    crossed, gbase, glayer, gw, gbias = pl.pallas_call(
        finish,
        out_shape=shapes,
        in_specs=[vmem] * 5,
        out_specs=(pl.BlockSpec(memory_space=pl.ANY),) * 5,
        scratch_shapes=[pltpu.SemaphoreType.DMA((8,))],
        compiler_params=pltpu.CompilerParams(vmem_limit_bytes=4 << 20),
        name="finish",
    )(*results)
    return crossed, gbase, glayer, gw.reshape(1024, 128), gbias.reshape(128)


def solution(mesh):
    return jax.shard_map(
        local,
        mesh=mesh,
        in_specs=(P("dp", "mp"), P("dp", "mp"), P(None, "mp"), P("mp"), P("dp", "mp")),
        out_specs=(P("dp", "mp"), P("dp", "mp"), P("dp", "mp"), P("dp", "mp"), P("mp")),
        check_vma=False,
    )
```

```python
import functools
import math

import jax
import jax.numpy as jnp
from jax import lax
from jax.experimental import pallas as pl
from jax.experimental.pallas import tpu as pltpu
from jax.sharding import PartitionSpec as P

MESH = pl.DeviceIdType.MESH
F32 = jnp.float32
BF16 = jnp.bfloat16
N_SENDS = 14
N_RECVS = 50
MOST_ROWS = 4096


def kernel(
    scale,
    base_hbm,
    lay_hbm,
    up_hbm,
    bias_hbm,
    w4,
    crossed,
    gbase,
    glayer,
    gw,
    gbias,
    base,
    lay,
    up,
    bias,
    wo,
    wp,
    dl,
    dlp,
    xa,
    fs,
    xb,
    do,
    dp_,
    bs,
    part,
    r1lo,
    r1hi,
    rl,
    rr,
    s1,
    b2s,
    r2,
    tt,
    zs,
    zr,
    mixp,
    mixr,
    gws,
    tally,
    send,
    recv,
    lsem,
):
    d = lax.axis_index("dp")
    m = lax.axis_index("mp")
    c = lax.rem(m, 2)
    y = lax.rem(lax.div(m, 2), 4)
    h = lax.rem(lax.div(m, 8), 2)
    x = lax.div(m, 16)
    oh = 1 - h
    oc = 1 - c

    def dev(x_=None, y_=None, h_=None, c_=None, d_=None):
        x_ = x if x_ is None else x_
        y_ = y if y_ is None else y_
        h_ = h if h_ is None else h_
        c_ = c if c_ is None else c_
        d_ = d if d_ is None else d_
        return (d_, ((x_ * 2 + h_) * 4 + y_) * 2 + c_)

    def plus(v, k):
        return lax.rem(v + k, 4)

    ids = iter(range(N_RECVS))
    send_ids = iter(range(N_SENDS))
    sent = [[next(send_ids), 0]]

    def rows(ref):
        return math.prod(ref.shape) * jnp.dtype(ref.dtype).itemsize // 256

    def wait_rows(sem, n):
        view = tally.at[pl.ds(0, n)]
        pltpu.make_async_copy(view, view, sem).wait()

    def put(src, dst, to, k=None):
        k = next(ids) if k is None else k
        n = rows(src)
        if sent[-1][1] + n > MOST_ROWS:
            sent.append([next(send_ids), 0])
        sent[-1][1] += n
        pltpu.make_async_remote_copy(
            src_ref=src,
            dst_ref=dst,
            send_sem=send.at[sent[-1][0]],
            recv_sem=recv.at[k],
            device_id=to,
            device_id_type=MESH,
        ).start()
        return k

    def got(k, *landed):
        wait_rows(recv.at[k], sum(rows(ref) for ref in landed))

    b4, b2, b1 = lax.div(d, 4), lax.rem(lax.div(d, 2), 2), lax.rem(d, 2)

    def first_row(d_, h_):
        window = jnp.clip(d_ - 2, 0, 4)
        return jnp.where(lax.rem(d_, 2) == h_, window, window + 4)

    barrier = pltpu.get_barrier_semaphore()
    near = []
    z = h * 8 + d
    for k in (8, 7, 9, 6, 10, 5, 11, 4, 12, 3, 13, 2, 14, 1, 15):
        zk = lax.rem(z + k, 16)
        near.append(dev(h_=lax.div(zk, 8), d_=lax.rem(zk, 8)))
    near += [dev(x_=plus(x, k)) for k in (2, 1, 3)]
    near += [dev(y_=plus(y, k)) for k in (2, 1, 3)]
    near.append(dev(c_=oc))
    for to in near:
        pl.semaphore_signal(barrier, inc=1, device_id=to, device_id_type=MESH)

    loads = [
        pltpu.make_async_copy(src, dst, lsem.at[k])
        for k, (src, dst) in enumerate(
            (
                (lay_hbm, lay),
                (up_hbm, up),
                (base_hbm, base),
                (lay_hbm, xa.at[h, x, y]),
                (bias_hbm, bias),
                (w4.at[:, :, :, c], wo),
            )
        )
    ]
    for load in loads:
        load.start()
    loads[0].wait()
    pl.semaphore_wait(barrier, len(near))

    def ag1(view, n):
        half = n // 2
        a = view(x, y, 0, half)
        b = view(x, y, half, half)
        k = next(ids)
        for j in (1, 3, 2):
            put(a, a, dev(x_=plus(x, j)), k)
            put(b, b, dev(y_=plus(y, j)), k)
        ks = []
        for j in (1, 3):
            ks.append((put(a, a, dev(y_=plus(y, j))), put(b, b, dev(x_=plus(x, j)))))
        return k, ks

    every = pl.ds(0, 4)

    def ag2(view, n, sent1):
        half = n // 2
        k, ks = sent1
        got(k, *[view(x, y, 0, half)] * 3, *[view(x, y, half, half)] * 3)
        for (ka, kb), j in zip(ks, (1, 3), strict=True):
            for i in (1, 3, 2):
                a = view(plus(x, i), y, 0, half)
                b = view(x, plus(y, i), half, half)
                put(a, a, dev(y_=plus(y, j)), ka)
                put(b, b, dev(x_=plus(x, j)), kb)
        return ks

    def ag2_forward(view, n, ks):
        half = n // 2
        k = next(ids)
        for (ka, kb), j, part_of in zip(ks, (1, 3), (pl.ds(0, 2), pl.ds(2, 2)), strict=True):
            ys, xs = plus(y, 4 - j), plus(x, 4 - j)
            got(ka, view(every, ys, 0, half))
            a = view(part_of, ys, 0, half)
            put(a, a, dev(y_=plus(y, j)), k)
            got(kb, view(xs, every, half, half))
            b = view(xs, part_of, half, half)
            put(b, b, dev(x_=plus(x, j)), k)
        return k

    def ag2_wait(view, n, k):
        half = n // 2
        got(k, view(every, y, 0, half), view(x, every, half, half))

    def x_own(xs, ys, q, nq):
        return xa.at[h, xs, ys, pl.ds(q, nq)]

    def x_other(xs, ys, q, nq):
        return xa.at[oh, xs, ys, pl.ds(q, nq)]

    def x_block0(xs, ys, q, nq):
        return xb.at[xs, ys, pl.ds(q, nq)]

    def x_block1(xs, ys, q, nq):
        return xb.at[xs, ys, pl.ds(4 + q, nq)]

    k_zx = put(lay, xa.at[h, x, y], dev(h_=oh))
    k_fs = next(ids)
    for j in (2, 1, 3):
        t = plus(x, j)
        put(lay.at[t], fs.at[x], dev(x_=t), k_fs)
    z_first = [next(send_ids) for _ in range(8)]
    z_recv = next(ids)
    next(ids)
    z_sent = []

    def along_z_to_block(j):
        s = plus(x, j)
        src = lay.at[x] if j == 0 else fs.at[s]
        d_to = 2 * s + h
        for hh in (0, 1):
            n = 2 * j + hh
            same = jnp.logical_and(h == hh, d_to == d)
            slot = lax.rem(d + 8 - first_row(d_to, hh), 8)
            dst = xb.at[x, y, slot]
            copy = pltpu.make_async_remote_copy(
                src_ref=src,
                dst_ref=dst,
                send_sem=send.at[z_first[n]],
                recv_sem=recv.at[z_recv + lax.div(slot, 4)],
                device_id=dev(h_=hh, d_=d_to),
                device_id_type=MESH,
            )
            stay = pltpu.make_async_copy(src, dst, recv.at[z_recv + lax.div(slot, 4)])

            @pl.when(same)
            def _(stay=stay):
                stay.start()

            @pl.when(jnp.logical_not(same))
            def _(copy=copy):
                copy.start()

            z_sent.append((same, copy))

    along_z_to_block(0)

    k_wp = [put(w4.at[:, oh, :, oc], wp.at[:, oh], dev(c_=oc))]
    loads[3].wait()
    own1 = ag1(x_own, 4)

    loads[1].wait()
    loads[2].wait()
    upper = up[...].astype(F32)
    basef = base[...].astype(F32)
    delta = upper * basef
    low = delta.astype(BF16).reshape(4, 32, 128)
    dl[...] = low
    do[:, b4, b2, b1] = low
    bs[b4, b2, b1] = jnp.broadcast_to(jnp.sum(delta, axis=0, keepdims=True), (8, 128))
    k_dlp = put(dl, dlp, dev(c_=oc))

    every2 = pl.ds(0, 2)
    steps = (
        (dev(d_=d + 4 - 8 * b4), (b4, b2, b1), (1 - b4, b2, b1)),
        (dev(d_=d + 2 - 4 * b2), (every2, b2, b1), (every2, 1 - b2, b1)),
        (dev(d_=d + 1 - 2 * b1), (every2, every2, b1), (every2, every2, 1 - b1)),
    )

    def along_z(step):
        to, here, _ = steps[step]
        a, b = do.at[(slice(None), *here)], bs.at[here]
        return put(b, b, to, put(a, a, to))

    def along_z_wait(step, k):
        theirs = steps[step][2]
        got(k, do.at[(slice(None), *theirs)], bs.at[theirs])

    k_d = along_z(0)
    k_wp.append(put(w4.at[:, h, :, oc], wp.at[:, h], dev(c_=oc)))

    loads[5].wait()
    got(k_dlp, dlp)
    d_own = dl[...].reshape(128, 128)
    d_other = dlp[...].reshape(128, 128)
    nt = (((1,), (1,)), ((), ()))
    lo, hi = pl.ds(0, 2), pl.ds(2, 2)

    def to_line(half, j):
        return dev(x_=plus(x, j)) if half == 0 else dev(y_=plus(y, j))

    def to_line2(half, j):
        return dev(y_=plus(y, j)) if half == 0 else dev(x_=plus(x, j))

    def back_terms(hs):
        for xs in range(4):
            term = lax.dot_general(
                wo[xs, hs].reshape(512, 128), d_own, nt, preferred_element_type=F32
            ) + lax.dot_general(
                wp[xs, hs].reshape(512, 128), d_other, nt, preferred_element_type=F32
            )
            term = term.astype(BF16).reshape(4, 128, 128)
            part[hs, 0, xs] = term[:, 0:64]
            for ys in range(4):
                part[hs, 1, ys, xs] = term[ys, 64:128]

    def rs1(hs):
        first, rest = [], next(ids)
        for half in (0, 1):
            me = x if half == 0 else y
            a = put(part.at[hs, half, plus(me, 2), lo], r1lo.at[hs, half], to_line(half, 1))
            b = put(part.at[hs, half, plus(me, 2), hi], r1hi.at[hs, half], to_line(half, 3))
            first.append((a, b))
        for half in (0, 1):
            me = x if half == 0 else y
            put(part.at[hs, half, plus(me, 1), hi], rl.at[hs, half, hi], to_line(half, 1), rest)
            put(part.at[hs, half, plus(me, 3), lo], rr.at[hs, half, lo], to_line(half, 3), rest)
        return first, rest

    def rs2(hs, ks):
        first, rest = ks
        for half in (0, 1):
            me = x if half == 0 else y
            a, b = first[half]
            got(a, r1lo.at[hs, half])
            t = plus(me, 1)
            part[hs, half, t, lo] = (
                part[hs, half, t, lo].astype(F32) + r1lo[hs, half].astype(F32)
            ).astype(BF16)
            put(part.at[hs, half, t, lo], rl.at[hs, half, lo], to_line(half, 1), rest)
            got(b, r1hi.at[hs, half])
            t = plus(me, 3)
            part[hs, half, t, hi] = (
                part[hs, half, t, hi].astype(F32) + r1hi[hs, half].astype(F32)
            ).astype(BF16)
            put(part.at[hs, half, t, hi], rr.at[hs, half, hi], to_line(half, 3), rest)
        return rest

    def rs3(hs, rest):
        got(rest, rl.at[hs], rr.at[hs])
        k = next(ids)
        for half in (0, 1):
            me, me2 = (x, y) if half == 0 else (y, x)
            total = (
                part[hs, half, me].astype(F32)
                + rl[hs, half].astype(F32)
                + rr[hs, half].astype(F32)
            )
            s1[hs, half] = total
            b2s[hs, half] = total.astype(BF16)
            for j in (1, 3, 2):
                t = plus(me2, j)
                put(b2s.at[hs, half, t], r2.at[hs, half, j - 1], to_line2(half, j), k)
        return k

    def rs4(hs, k):
        got(k, r2.at[hs])
        for half in (0, 1):
            me2 = y if half == 0 else x
            tt[hs, half] = (
                s1[hs, half, me2]
                + r2[hs, half, 0].astype(F32)
                + r2[hs, half, 1].astype(F32)
                + r2[hs, half, 2].astype(F32)
            )

    got(k_wp[0], wp.at[:, oh])
    back_terms(oh)
    k_far = rs1(oh)
    got(k_wp[1], wp.at[:, h])
    back_terms(h)
    k_near = rs1(h)

    got(k_fs, lay.at[pl.ds(0, 3)])
    for j in (1, 2, 3):
        along_z_to_block(j)
    own2 = ag2(x_own, 4, own1)
    k_far = rs2(oh, k_far)
    k_near = rs2(h, k_near)

    def mixed_terms(hs, acc):
        for xs in range(4):
            rows = jnp.concatenate([xa[hs, xs, ys].reshape(128, 128) for ys in range(4)], axis=1)
            cols = jnp.concatenate(
                [wo[xs, hs].reshape(512, 128), wp[xs, hs].reshape(512, 128)], axis=1
            )
            acc = acc + jnp.dot(rows, cols, preferred_element_type=F32)
        return acc

    quarter = xb.at[x, y, pl.ds(0, 4)]
    got(z_recv, quarter)
    first1 = ag1(x_block0, 4)
    got(k_zx, xa.at[oh, x, y])
    other1 = ag1(x_other, 4)
    own3 = ag2_forward(x_own, 4, own2)
    k_far = rs3(oh, k_far)
    along_z_wait(0, k_d)
    k_d = along_z(1)
    got(z_recv + 1, quarter)
    second1 = ag1(x_block1, 4)
    k_near = rs3(h, k_near)

    first2 = ag2(x_block0, 4, first1)
    other2 = ag2(x_other, 4, other1)
    along_z_wait(1, k_d)
    k_d = along_z(2)

    rs4(oh, k_far)
    zs[...] = tt[oh].astype(BF16)
    k_zr = put(zs, zr, dev(h_=oh))

    second2 = ag2(x_block1, 4, second1)
    ag2_wait(x_own, 4, own3)
    mixp[...] = mixed_terms(h, jnp.zeros((128, 256), F32))

    first3 = ag2_forward(x_block0, 4, first2)
    other3 = ag2_forward(x_other, 4, other2)
    rs4(h, k_near)
    second3 = ag2_forward(x_block1, 4, second2)
    along_z_wait(2, k_d)
    k_dp = put(do, dp_, dev(c_=oc))

    ag2_wait(x_other, 4, other3)
    mixp[...] = mixed_terms(oh, mixp[...])
    k_mix = put(mixp.at[:, pl.ds(128, 128)], mixr, dev(c_=oc))


    def rows_of(ref, xs, g):
        out = []
        for k in range(4):
            s = lax.rem(first_row(d, h) + 4 * g + k, 8)
            out.append(ref[xs, lax.div(s, 4), lax.rem(lax.div(s, 2), 2), lax.rem(s, 2)])
        return jnp.concatenate(out, axis=0)

    def features(g):
        return jnp.concatenate(
            [
                jnp.concatenate(
                    [xb[xs, ys, 4 * g : 4 * g + 4].reshape(128, 128) for ys in range(4)], axis=1
                ).T
                for xs in range(4)
            ],
            axis=1,
        )

    def weight_terms(feats, g, ref):
        cols = jnp.concatenate([rows_of(ref, xs, g) for xs in range(4)], axis=0)
        return jnp.dot(feats, cols, preferred_element_type=F32)

    got(k_dp, dp_)
    ag2_wait(x_block0, 4, first3)
    feats = features(0)
    gws[...] = weight_terms(feats, 0, dp_).reshape(4, 128, 128)
    gw[:, c] = weight_terms(feats, 0, do).reshape(4, 128, 128)
    ag2_wait(x_block1, 4, second3)
    feats = features(1)
    gws[...] = (gws[...] + weight_terms(feats, 1, dp_).reshape(4, 128, 128)) * scale
    k_gw = put(gws, gw.at[:, c], dev(c_=oc))
    gw[:, c] = (gw[:, c] + weight_terms(feats, 1, do).reshape(4, 128, 128)) * scale

    gbias[...] = jnp.sum(bs[...].reshape(8, 8, 128)[:, 0], axis=0, keepdims=True) * scale

    got(k_mix, mixr)
    loads[4].wait()
    mixed = mixp[:, 0:128] + mixr[...] + bias[...]
    crossed[...] = (basef * mixed + lay[...].reshape(128, 128).astype(F32)).astype(BF16)
    gbase[...] = (upper * mixed).astype(BF16)

    got(k_zr, zr)
    back = (tt[h] + zr[...].astype(F32)).reshape(128, 128)
    glayer[...] = (upper + back.T).astype(BF16)

    got(k_gw, gw.at[:, oc])
    for k, n in sent:
        wait_rows(send.at[k], n)
    for same, copy in z_sent:

        @pl.when(jnp.logical_not(same))
        def _(copy=copy):
            copy.wait_send()


def finish(a, b, e, g, s, oa, ob, oe, og, os_, sem):
    copies = [
        pltpu.make_async_copy(src, dst, sem.at[k])
        for k, (src, dst) in enumerate(
            (
                (g.at[0], og.at[0]),
                (g.at[1], og.at[1]),
                (g.at[2], og.at[2]),
                (g.at[3], og.at[3]),
                (a, oa),
                (b, ob),
                (e, oe),
                (s, os_),
            )
        )
    ]
    for copy in copies:
        copy.start()
    for copy in copies:
        copy.wait()


def local(base_rows, layer_rows, cross_weight, cross_bias, upstream):
    vmem = pl.BlockSpec(memory_space=pltpu.VMEM)
    hbm = pl.BlockSpec(memory_space=pltpu.HBM)
    scale = float((base_rows.shape[0] * 8) ** -0.5)
    small = jax.ShapeDtypeStruct((128, 128), BF16)
    shapes = (
        small,
        small,
        small,
        jax.ShapeDtypeStruct((4, 2, 128, 128), F32),
        jax.ShapeDtypeStruct((1, 128), F32),
    )
    results = pl.pallas_call(
        functools.partial(kernel, scale),
        out_shape=shapes,
        in_specs=[hbm] * 5,
        out_specs=(vmem, vmem, vmem, vmem, vmem),
        scratch_shapes=[
            pltpu.VMEM((128, 128), BF16),
            pltpu.VMEM((4, 32, 128), BF16),
            pltpu.VMEM((128, 128), BF16),
            pltpu.VMEM((1, 128), F32),
            pltpu.VMEM((4, 2, 4, 128, 128), BF16),
            pltpu.VMEM((4, 2, 4, 128, 128), BF16),
            pltpu.VMEM((4, 32, 128), BF16),
            pltpu.VMEM((4, 32, 128), BF16),
            pltpu.VMEM((2, 4, 4, 4, 32, 128), BF16),
            pltpu.VMEM((4, 32, 128), BF16),
            pltpu.VMEM((4, 4, 8, 32, 128), BF16),
            pltpu.VMEM((4, 2, 2, 2, 32, 128), BF16),
            pltpu.VMEM((4, 2, 2, 2, 32, 128), BF16),
            pltpu.VMEM((2, 2, 2, 8, 128), F32),
            pltpu.VMEM((2, 2, 4, 4, 64, 128), BF16),
            pltpu.VMEM((2, 2, 2, 64, 128), BF16),
            pltpu.VMEM((2, 2, 2, 64, 128), BF16),
            pltpu.VMEM((2, 2, 4, 64, 128), BF16),
            pltpu.VMEM((2, 2, 4, 64, 128), BF16),
            pltpu.VMEM((2, 2, 4, 64, 128), F32),
            pltpu.VMEM((2, 2, 4, 64, 128), BF16),
            pltpu.VMEM((2, 2, 3, 64, 128), BF16),
            pltpu.VMEM((2, 2, 64, 128), F32),
            pltpu.VMEM((2, 64, 128), BF16),
            pltpu.VMEM((2, 64, 128), BF16),
            pltpu.VMEM((128, 256), F32),
            pltpu.VMEM((128, 128), F32),
            pltpu.VMEM((4, 128, 128), F32),
            pltpu.VMEM((2 * MOST_ROWS, 128), BF16),
            pltpu.SemaphoreType.DMA((N_SENDS,)),
            pltpu.SemaphoreType.DMA((N_RECVS,)),
            pltpu.SemaphoreType.DMA((6,)),
        ],
        compiler_params=pltpu.CompilerParams(
            collective_id=0, has_side_effects=True, vmem_limit_bytes=24 << 20
        ),
        name="cross_layer",
    )(
        *(
            pltpu.with_memory_space_constraint(a, pltpu.HBM)
            for a in (
                base_rows,
                layer_rows.reshape(4, 32, 128),
                upstream,
                cross_bias.reshape(1, 128),
                cross_weight.reshape(4, 2, 4, 2, 128, 128),
            )
        )
    )
    crossed, gbase, glayer, gw, gbias = pl.pallas_call(
        finish,
        out_shape=shapes,
        in_specs=[vmem] * 5,
        out_specs=(pl.BlockSpec(memory_space=pl.ANY),) * 5,
        scratch_shapes=[pltpu.SemaphoreType.DMA((8,))],
        compiler_params=pltpu.CompilerParams(vmem_limit_bytes=4 << 20),
        name="finish",
    )(*results)
    return crossed, gbase, glayer, gw.reshape(1024, 128), gbias.reshape(128)


def solution(mesh):
    return jax.shard_map(
        local,
        mesh=mesh,
        in_specs=(P("dp", "mp"), P("dp", "mp"), P(None, "mp"), P("mp"), P("dp", "mp")),
        out_specs=(P("dp", "mp"), P("dp", "mp"), P("dp", "mp"), P("dp", "mp"), P("mp")),
        check_vma=False,
    )
```
